512 devices in a mesh: leaf: 16 (over y, x), box: 32 (over z, core).
Axes of the slice: x: 4, y: 4, z: 16, core: 2. Of those that a mesh axis runs over, the one named last changes fastest.
Arguments:
- krylov_block: float32 [64, 524288], P(None, ('leaf', 'box')), as said below
- bases: float32 [32, 524288], P(None, ('leaf', 'box')), may hold values from -0.5 to 0.5
- points: float32 [3, 524288], P(None, ('leaf', 'box')), may hold values from 0 to 1, as said below
- panel_size: float32 [524288], P(('leaf', 'box')), may hold values from 0.002 to 0.008
- panel_weight: float32 [524288], P(('leaf', 'box')), may hold values from 0.5 to 2
- near_list: int32 [4096, 16], P(('leaf', 'box')), may hold values from 0 to 4095, as said below
- far_list: int32 [4096, 12], P(('leaf', 'box')), may hold values from 0 to 4095, as said below
- far_class: int32 [4096, 12], P(('leaf', 'box')), may hold values from 0 to 15
- far_count: int32 [4096], P(('leaf', 'box')), may hold values from 1 to 12
- coarse_list: int32 [512, 16], P(('leaf', 'box')), may hold values from 0 to 511, as said below
- coarse_class: int32 [512, 16], P(('leaf', 'box')), may hold values from 0 to 15
- coarse_count: int32 [512], P(('leaf', 'box')), may hold values from 1 to 16
- couple_fine: float32 [16, 32, 32], replicated, may hold values from -0.3125 to 0.3125
- couple_coarse: float32 [16, 32, 32], replicated, may hold values from -1 to 1
- up_transfer: float32 [8, 32, 32], replicated, may hold values from -0.375 to 0.375
- down_transfer: float32 [8, 32, 32], replicated, may hold values from -1 to 1
Outputs:
- basis_next: float32 [64, 524288], P(None, ('leaf', 'box'))
- hessenberg: float32 [64, 64], replicated
- factor: float32 [64, 64], replicated
The draws below stay inside these ranges and needn't reach their ends.
Inputs may be any that keep to these rules, and one draw needn't show every extreme that they name: `near_list`: entry 0 of a box's row is the box itself. Every entry lies in the box's own group of 256 consecutive boxes (groups aligned), and at most 8 boxes before the first or after the last box of the box's aligned block of 8 boxes. `far_list`: every entry lies in the box's own aligned group of 256 consecutive boxes. `coarse_list`: entries may name any parent. `krylov_block`: rows differ in scale. `points`: the panels of leaf box b lie in the cell of a regular grid of the unit cube that the Morton code b names (bit k of b counts along coordinate k mod 3).
All inputs are finite; a program needn't handle non-finite values.
Results may differ from the reference program's by a relative error of at most 0.0025.
Values sent between devices are 32-bit elements; how exact they have to be, the bound alone decides.
No kernel may reach another device: no remote copies, remote signals or barrier semaphores. Data moves between devices by JAX's collectives and lax.ppermute only.
A program may use at most 64 MiB of HBM per device.

```python
import math
import jax
import jax.numpy as jnp
from jax import lax

RHS = 64
RANK = 32
M = 128
CHILDREN = 8
NEAR = 16
FAR1 = 12
FAR2 = 16
CLASSES = 16
PARENTS = 512
BOXES = 4096
SUB_BOXES = 256
PANELS = 524288


def draw_krylov_block(key, part):
    position = jnp.arange(PANELS, dtype=jnp.float32) / PANELS
    return jax.random.normal(key, (RHS, PANELS), jnp.float32) * (1.0 + 2.0 * position)


def draw_points(key, part):
    box_ids = jnp.arange(PANELS, dtype=jnp.int32) // M
    bit_total = BOXES.bit_length() - 1
    cells = [jnp.zeros((PANELS,), jnp.int32) for axis_number in range(3)]
    extents = [1, 1, 1]
    for bit_number in range(bit_total):
        axis_number = bit_number % 3
        bit_value = box_ids // 2 ** bit_number % 2
        cells[axis_number] = cells[axis_number] + bit_value * 2 ** (bit_number // 3)
        extents[axis_number] = extents[axis_number] * 2
    inside = jax.random.uniform(jax.random.fold_in(key, 31), (3, PANELS), jnp.float32, 0.0, 1.0)
    rows = [(cells[axis_number].astype(jnp.float32) + inside[axis_number]) / extents[axis_number] for axis_number in range(3)]
    return jnp.clip(jnp.stack(rows, 0), 0.0, 1.0)


def draw_near_list(key, part):
    box_ids = jnp.arange(BOXES, dtype=jnp.int32)
    block_first = box_ids // CHILDREN * CHILDREN
    group_first = box_ids // SUB_BOXES * SUB_BOXES
    offsets = jax.random.randint(jax.random.fold_in(key, 11), (BOXES, NEAR - 1), 0, 3 * CHILDREN, dtype=jnp.int32)
    candidate = block_first[:, None] - CHILDREN + offsets
    candidate = jnp.clip(candidate, group_first[:, None], group_first[:, None] + SUB_BOXES - 1)
    return jnp.concatenate([box_ids[:, None], candidate], axis=1).astype(jnp.int32)


def draw_far_list(key, part):
    box_ids = jnp.arange(BOXES, dtype=jnp.int32)
    group_first = box_ids // SUB_BOXES * SUB_BOXES
    offsets = jax.random.randint(jax.random.fold_in(key, 23), (BOXES, FAR1), 0, SUB_BOXES, dtype=jnp.int32)
    return (group_first[:, None] + offsets).astype(jnp.int32)


def draw_coarse_list(key, part):
    parent_ids = jnp.arange(PARENTS, dtype=jnp.int32)
    previous = (parent_ids + PARENTS - 1) % PARENTS
    opposite = (parent_ids + PARENTS // 2) % PARENTS
    others = jax.random.randint(jax.random.fold_in(key, 37), (PARENTS, FAR2 - 2), 0, PARENTS, dtype=jnp.int32)
    return jnp.concatenate([previous[:, None], opposite[:, None], others], axis=1).astype(jnp.int32)


def plant(entries, stream_key, low, high):
    shape = entries.shape
    spot = [jax.random.randint(jax.random.fold_in(stream_key, axis), (), 0, shape[axis]) for axis in range(len(shape))]
    entries = entries.at[tuple(spot)].set(low)
    longest = shape.index(max(shape))
    spot[longest] = (spot[longest] + 1) % shape[longest]
    return entries.at[tuple(spot)].set(high)


def shard_levels(stream_key, dims, cuts, least, largest):
    def one(dim, shards_of):
        steps = jax.random.uniform(jax.random.fold_in(jax.random.fold_in(stream_key, 6), dim), (shards_of,), jnp.float32, least / len(cuts), largest / len(cuts))
        return jnp.repeat(jnp.exp(steps), dims[dim] // shards_of).reshape((-1,) + (1,) * (len(dims) - dim - 1))

    loudness = one(*cuts[0])
    for cut in cuts[1:]:
        loudness = loudness * one(*cut)
    return loudness


def noise(rng, extent, scale, most, pieces=(), held_as=jnp.bfloat16):
    values = scale * jax.random.normal(rng, extent, jnp.float32)
    if pieces:
        values = values * shard_levels(rng, extent, pieces, -0.22, 0.18)
    return jnp.clip(values, -most, most).astype(held_as)


def setup_inputs(seed: int = 0) -> dict:
    key_list = jax.random.split(jax.random.key(seed), 17)
    return {
        "krylov_block": draw_krylov_block(jax.random.fold_in(key_list[16], 71), 0),
        "bases": noise(key_list[1], (RANK, PANELS), M ** -0.5, 0.5, ((1, 512),), jnp.float32),
        "points": draw_points(jax.random.fold_in(key_list[16], 71), 0),
        "panel_size": jnp.clip(jnp.exp(math.log(0.008) - 1.3862944 * jax.random.uniform(key_list[3], (PANELS,), jnp.float32) ** shard_levels(key_list[3], (PANELS,), ((0, 512),), -0.2, 0.2)), 0.002, 0.008),
        "panel_weight": jnp.clip(jnp.exp(math.log(2.0) - 1.3862944 * jax.random.uniform(key_list[4], (PANELS,), jnp.float32) ** shard_levels(key_list[4], (PANELS,), ((0, 512),), -0.2, 0.2)), 0.5, 2.0),
        "near_list": draw_near_list(jax.random.fold_in(key_list[16], 71), 0),
        "far_list": draw_far_list(jax.random.fold_in(key_list[16], 71), 0),
        "far_class": plant(jax.random.randint(key_list[7], (BOXES, FAR1), 0, CLASSES), jax.random.fold_in(key_list[7], 1), 0, CLASSES - 1).astype(jnp.int32),
        "far_count": plant(jax.random.randint(key_list[8], (BOXES,), 1, FAR1 + 1), jax.random.fold_in(key_list[8], 1), 1, FAR1).astype(jnp.int32),
        "coarse_list": draw_coarse_list(jax.random.fold_in(key_list[16], 71), 0),
        "coarse_class": plant(jax.random.randint(key_list[10], (PARENTS, FAR2), 0, CLASSES), jax.random.fold_in(key_list[10], 1), 0, CLASSES - 1).astype(jnp.int32),
        "coarse_count": plant(jax.random.randint(key_list[11], (PARENTS,), 1, FAR2 + 1), jax.random.fold_in(key_list[11], 1), 1, FAR2).astype(jnp.int32),
        "couple_fine": noise(key_list[12], (CLASSES, RANK, RANK), (RANK * FAR1) ** -0.5, 0.3125, (), jnp.float32),
        "couple_coarse": noise(key_list[13], (CLASSES, RANK, RANK), RANK ** -0.5, 1.0, (), jnp.float32),
        "up_transfer": noise(key_list[14], (CHILDREN, RANK, RANK), (RANK * CHILDREN) ** -0.5, 0.375, (), jnp.float32),
        "down_transfer": noise(key_list[15], (CHILDREN, RANK, RANK), RANK ** -0.5, 1.0, (), jnp.float32),
    }


HIGHEST_PRECISION = lax.Precision.HIGHEST

def pairwise(target, source, source_values, scale_count):
    first = target[0][:, None] - source[0][None, :]
    second = target[1][:, None] - source[1][None, :]
    third = target[2][:, None] - source[2][None, :]
    squared = first * first + second * second + third * third
    green = source[4][None, :] / (scale_count * jnp.sqrt(squared + target[3][:, None] * source[3][None, :]))
    return jnp.dot(source_values, green.T, precision=HIGHEST_PRECISION)

def reference(krylov_block, bases, points, panel_size, panel_weight, near_list, far_list, far_class, far_count, coarse_list, coarse_class, coarse_count, couple_fine, couple_coarse, up_transfer, down_transfer):
    block_values = krylov_block.reshape(RHS, BOXES, M)
    block_basis = bases.reshape(RANK, BOXES, M)
    geometry = jnp.concatenate([points, panel_size[None, :], panel_weight[None, :]], 0).reshape(5, BOXES, M)
    fine_poles = jnp.einsum('rbm,qbm->brq', block_basis, block_values, precision=HIGHEST_PRECISION)
    grouped = fine_poles.reshape(PARENTS, CHILDREN, RANK, RHS)
    coarse_poles = jnp.einsum('ckr,pckq->prq', up_transfer, grouped, precision=HIGHEST_PRECISION)
    live_coarse = (jnp.arange(FAR2, dtype=jnp.int32)[None, :] < coarse_count[:, None]).astype(jnp.float32)
    coarse_matrices = couple_coarse[coarse_class] * live_coarse[:, :, None, None]
    coarse_local = jnp.einsum('perk,pekq->prq', coarse_matrices, coarse_poles[coarse_list], precision=HIGHEST_PRECISION)

    def per_box(box_index):
        sources = near_list[box_index]
        source_geometry = geometry[:, sources].reshape(5, NEAR * M)
        source_values = block_values[:, sources].reshape(RHS, NEAR * M)
        near_field = pairwise(geometry[:, box_index], source_geometry, source_values, M * NEAR)
        live_mask = (jnp.arange(FAR1, dtype=jnp.int32) < far_count[box_index]).astype(jnp.float32)
        matrices = couple_fine[far_class[box_index]] * live_mask[:, None, None]
        fine_local = jnp.einsum('erk,ekq->rq', matrices, fine_poles[far_list[box_index]], precision=HIGHEST_PRECISION)
        fine_local = fine_local + jnp.dot(down_transfer[box_index % CHILDREN], coarse_local[box_index // CHILDREN], precision=HIGHEST_PRECISION)
        far_field = jnp.dot(fine_local.T, block_basis[:, box_index], precision=HIGHEST_PRECISION)
        return near_field + far_field
    product = lax.map(per_box, jnp.arange(BOXES, dtype=jnp.int32))
    product = product.transpose(1, 0, 2).reshape(RHS, PANELS)
    hessenberg = jnp.dot(krylov_block, product.T, precision=HIGHEST_PRECISION) / PANELS
    residual = product - jnp.dot(hessenberg.T, krylov_block, precision=HIGHEST_PRECISION)
    gram_matrix = jnp.dot(residual, residual.T, precision=HIGHEST_PRECISION) / PANELS
    factor = jnp.linalg.cholesky(gram_matrix)
    basis_next = lax.linalg.triangular_solve(factor, residual, left_side=True, lower=True)
    return (basis_next, hessenberg, factor)
```

```python
import jax
import jax.numpy as jnp
from jax import lax
from jax.experimental import pallas as pl
from jax.experimental.pallas import tpu as pltpu
from jax.sharding import Mesh
from jax.sharding import PartitionSpec as P

LEAF = ("leaf_0", "leaf_1")
BOX = ("box_0", "box_1")
LEAF_BOX = LEAF + BOX
PLANE = ("leaf_0", "leaf_1", "box_1")
F32 = jnp.float32
BF16 = jnp.bfloat16
HI = lax.Precision.HIGHEST
NT = (((1,), (1,)), ((), ()))
TN = (((0,), (0,)), ((), ()))

Q = 64
R = 32
M = 128
C = 8
NEAR = 16
FAR1 = 12
FAR2 = 16
D = 32
W = C * M


def nn(a, b):
    return jnp.dot(a, b, precision=HI, preferred_element_type=F32)


def nt(a, b):
    return lax.dot_general(a, b, NT, precision=HI, preferred_element_type=F32)


def tn(a, b):
    return lax.dot_general(a, b, TN, precision=HI, preferred_element_type=F32)


def bdot(a, b):
    return jnp.dot(a, b, preferred_element_type=F32)


def halves(x):
    hi = x.astype(BF16)
    return hi, (x - hi.astype(F32)).astype(BF16)


def lane_flat(x, rows, width):
    wide = jnp.concatenate([x] * rows + [jnp.zeros((rows, 128 - rows * width), F32)], axis=1)
    lane = lax.broadcasted_iota(jnp.int32, (rows, 128), 1)
    row = lax.broadcasted_iota(jnp.int32, (rows, 128), 0)
    keep = (lane >= row * width) & (lane < (row + 1) * width)
    return jnp.sum(jnp.where(keep, wide, 0.0), axis=0, keepdims=True)


def poles_kernel(
    far_count, coarse_count, v_ref, b_ref, up_ref, far_list, far_class, coarse_list, coarse_class, out_ref
):
    parts = []
    coarse = jnp.zeros((Q, R), F32)
    for b in range(C):
        cols = slice(b * M, (b + 1) * M)
        pole = nt(v_ref[:, cols], b_ref[:, cols])
        coarse = coarse + nn(pole, up_ref[b])
        parts.append(pole)
    for half in range(2):
        rows = slice(half * D, (half + 1) * D)
        for t in range(2):
            out_ref[:, 2 * half + t, :] = jnp.concatenate([p[rows] for p in parts[4 * t : 4 * t + 4]], axis=1)
    slot = lax.broadcasted_iota(jnp.int32, (C, FAR1), 1)
    row = lax.broadcasted_iota(jnp.int32, (C, FAR1), 0)
    live = jnp.zeros((C, FAR1), jnp.int32)
    for b in range(C):
        live = jnp.where(row == b, far_count[b], live)
    box = far_list[...] & 255
    place = ((box & 7) * D + (box >> 3)).astype(F32)
    place = jnp.where(slot < live, place, -1.0)
    out_ref[:, 5, :] = jnp.broadcast_to(lane_flat(place, C, FAR1), (D, 128))
    out_ref[:, 6, :] = jnp.broadcast_to(lane_flat(far_class[...].astype(F32), C, FAR1), (D, 128))
    parent = coarse_list[...]
    inner = parent & 31
    spot = ((parent >> 5) * 16 + (inner & 15) + (inner >> 4) * 256).astype(F32)
    spot = jnp.where(lax.broadcasted_iota(jnp.int32, (1, FAR2), 1) < coarse_count[0], spot, -1.0)
    tail = jnp.concatenate(
        [spot, coarse_class[...].astype(F32), jnp.zeros((1, 128 - 64 - 2 * FAR2), F32)], axis=1
    )
    out_ref[:, 4, :] = jnp.concatenate(
        [coarse[:D], coarse[D:], jnp.broadcast_to(tail, (D, 64))], axis=1
    )


def near_kernel(index, left, own, right, out_ref, geo, vhi, vlo):
    for part, ref in enumerate((left, own, right)):
        for s in range(C):
            cols = slice(s * M, (s + 1) * M)
            turned = jnp.transpose(ref[Q : Q + 8, cols])
            for k in range(4):
                geo[part * C + s, k] = jnp.broadcast_to(turned[:, k : k + 1], (M, M))
            value = ref[:Q, cols] * (ref[Q + 4 : Q + 5, cols] * (1.0 / (M * NEAR)))
            hi, lo = halves(value)
            vhi[part * C + s] = hi
            vlo[part * C + s] = lo
    base = index[0, 0] - C

    def one_box(b, carry):
        cols = pl.ds(pl.multiple_of(b * M, M), M)
        target = [own[Q + k : Q + k + 1, cols] for k in range(4)]
        acc = jnp.zeros((Q, M), F32)
        for pair in range(NEAR // 2):
            ghi = []
            glo = []
            at = [index[b, 2 * pair + k] - base for k in range(2)]
            for i in at:
                d0 = geo[i, 0] - target[0]
                d1 = geo[i, 1] - target[1]
                d2 = geo[i, 2] - target[2]
                g = lax.rsqrt(d0 * d0 + d1 * d1 + d2 * d2 + geo[i, 3] * target[3])
                hi, lo = halves(g)
                ghi.append(hi)
                glo.append(lo)
            ghi = jnp.concatenate(ghi, axis=0)
            glo = jnp.concatenate(glo, axis=0)
            xhi = jnp.concatenate([vhi[i] for i in at], axis=1)
            xlo = jnp.concatenate([vlo[i] for i in at], axis=1)
            acc = acc + bdot(xhi, ghi) + (bdot(xlo, ghi) + bdot(xhi, glo))
        out_ref[:, cols] = acc
        return carry

    lax.fori_loop(0, C, one_box, 0)


def coarse_send_kernel(got_ref, out_ref):
    pole = got_ref[:, 4, :]
    both = jnp.concatenate([pole[:16, :64], pole[16:, :64]], axis=1)
    for k in range(16):
        out_ref[k] = both


def couple_tile(table, t):
    a = table[2 * t]
    b = table[2 * t + 1]
    zero = jnp.zeros((R, R), F32)
    return jnp.concatenate(
        [jnp.concatenate([a, zero, b, zero], axis=1), jnp.concatenate([zero, a, zero, b], axis=1)], axis=0
    )


def doubled(x):
    return x + pltpu.roll(x, 64, 1)


def fine_kernel(got_ref, table, out_ref, sel, cls):
    pieces = []
    for j in range(C):
        lanes = slice((j % 4) * R, (j % 4 + 1) * R)
        pieces.append(
            jnp.concatenate([got_ref[:, j // 4, :][:, lanes], got_ref[:, 2 + j // 4, :][:, lanes]], axis=1)
        )
    hi, lo = halves(jnp.concatenate(pieces, axis=0))
    source = jnp.concatenate([hi, lo], axis=1)
    place = got_ref[:, 5, :]
    kind = got_ref[:, 6, :]
    lane = lax.broadcasted_iota(jnp.int32, (D, C * D), 1).astype(F32)
    for e in range(FAR1):
        hot = []
        for j in range(C):
            k = j * FAR1 + e
            hot.append(jnp.where(jnp.broadcast_to(place[:, k : k + 1], (D, C * D)) == lane, 1.0, 0.0))
            cls[e, j * D : (j + 1) * D, :] = jnp.broadcast_to(kind[:, k : k + 1], (D, 128))
        sel[e] = doubled(bdot(jnp.concatenate(hot, axis=0).astype(BF16), source))
    odd = (lax.broadcasted_iota(jnp.int32, (C * D, 128), 1) >= 64).astype(F32)
    total = jnp.zeros((C * D, 64), F32)
    for t in range(8):
        which = odd + 2.0 * t
        z = jnp.zeros((C * D, 128), F32)
        for e in range(FAR1):
            z = z + jnp.where(cls[e] == which, sel[e], 0.0)
        total = total + nt(z, couple_tile(table, t))
    out_ref[...] = total


def coarse_kernel(got_ref, all_ref, table, down, fine_ref, out_ref):
    pole = all_ref[...].reshape(256, 128)
    hi, lo = halves(pole)
    source = jnp.concatenate(
        [
            jnp.concatenate([hi[:, :64], lo[:, :64]], axis=1),
            jnp.concatenate([hi[:, 64:], lo[:, 64:]], axis=1),
        ],
        axis=0,
    )
    listed = got_ref[:, 4, :]
    lane = lax.broadcasted_iota(jnp.int32, (D, 512), 1).astype(F32)
    hot = [
        jnp.where(jnp.broadcast_to(listed[:, 64 + e : 65 + e], (D, 512)) == lane, 1.0, 0.0)
        for e in range(FAR2)
    ]
    picked = doubled(bdot(jnp.concatenate(hot, axis=0).astype(BF16), source))
    odd = (lax.broadcasted_iota(jnp.int32, (D, 128), 1) >= 64).astype(F32)
    kinds = [
        jnp.broadcast_to(listed[:, 64 + FAR2 + e : 65 + FAR2 + e], (D, 128)) for e in range(FAR2)
    ]
    local = jnp.zeros((D, 64), F32)
    for t in range(8):
        which = odd + 2.0 * t
        z = jnp.zeros((D, 128), F32)
        for e in range(FAR2):
            z = z + jnp.where(kinds[e] == which, picked[e * D : (e + 1) * D], 0.0)
        local = local + nt(z, couple_tile(table, t))
    rows = []
    for j in range(C):
        turned = jnp.concatenate(
            [nt(local[:, :R], down[j]), nt(local[:, R:], down[j])], axis=1
        )
        rows.append(fine_ref[j * D : (j + 1) * D, :] + turned)
    for q in range(2):
        for h in range(2):
            out_ref[:, 2 * q + h, :] = jnp.concatenate(
                [rows[4 * h + k][:, q * R : (q + 1) * R] for k in range(4)], axis=1
            )


def product_kernel(got_ref, near_ref, v_ref, b_ref, out_ref, gram_ref):
    for b in range(C):
        cols = slice(b * M, (b + 1) * M)
        lanes = slice((b % 4) * R, (b % 4 + 1) * R)
        local = jnp.concatenate([got_ref[:, b // 4, :][:, lanes], got_ref[:, 2 + b // 4, :][:, lanes]], axis=0)
        out_ref[:, cols] = near_ref[:, cols] + nn(local, b_ref[:, cols])
    v = v_ref[...]
    image = out_ref[...]
    for k, g in enumerate((nt(v, v), nt(v, image), nt(image, image))):
        gram_ref[:, k, :] = jnp.concatenate([g[:D], g[D:]], axis=1)


def finish_kernel(got_ref, v_ref, p_ref, next_ref, hess_ref, factor_ref):
    panels = float(M * C * D * 16)
    grams = [
        jnp.concatenate([got_ref[:, k, :][:, :64], got_ref[:, k, :][:, 64:]], axis=0) for k in range(3)
    ]
    basis, mixed, image = grams
    hess = mixed * (1.0 / panels)
    hess_ref[...] = hess
    cross = tn(mixed, hess)
    gram = (image - cross - jnp.transpose(cross) + nn(tn(hess, basis), hess)) * (1.0 / panels)
    residual = p_ref[...] - tn(hess, v_ref[...])
    row = lax.broadcasted_iota(jnp.int32, (Q, Q), 0)
    col = lax.broadcasted_iota(jnp.int32, (Q, Q), 1)
    work = jnp.concatenate([gram, jnp.where(row == col, 1.0, 0.0)], axis=1)
    tiles = [work[8 * k : 8 * k + 8] for k in range(8)]
    sub = lax.broadcasted_iota(jnp.int32, (8, 128), 0)
    scales = [jnp.zeros((8, 128), F32) for k in range(8)]
    for j in range(Q):
        own = j // 8
        at = j % 8
        line = jnp.broadcast_to(tiles[own][at : at + 1], (8, 128))
        column = jnp.broadcast_to(tiles[own][:, j : j + 1], (8, 128))
        pivot = jnp.broadcast_to(column[at : at + 1], (8, 128))
        scaled = line / pivot
        scales[own] = jnp.where(sub == at, pivot, scales[own])
        tiles[own] = tiles[own] - jnp.where(sub > at, column, 0.0) * scaled
        for k in range(own + 1, 8):
            tiles[k] = tiles[k] - jnp.broadcast_to(tiles[k][:, j : j + 1], (8, 128)) * scaled
    whole = jnp.concatenate([tiles[k] * lax.rsqrt(scales[k]) for k in range(8)], axis=0)
    factor_ref[...] = jnp.transpose(jnp.where(col >= row, whole[:, :Q], 0.0))
    next_ref[...] = nn(whole[:, Q:], residual)


def sds(*shape):
    return jax.ShapeDtypeStruct(shape, F32)


SMEM = pl.BlockSpec(memory_space=pltpu.SMEM)
VMEM = pl.BlockSpec(memory_space=pltpu.VMEM)


def call(kernel, out, smem=0, vmem=0, scratch=(), name=None):
    return pl.pallas_call(
        kernel,
        out_shape=out,
        in_specs=[SMEM] * smem + [VMEM] * vmem,
        out_specs=jax.tree.map(lambda _: VMEM, out),
        scratch_shapes=list(scratch),
        compiler_params=pltpu.CompilerParams(vmem_limit_bytes=48 << 20),
        name=name,
    )


def exchange(blocks, axes):
    return lax.all_to_all(blocks, axes, 0, 0, tiled=True)


def per_device(
    krylov_block,
    bases,
    points,
    panel_size,
    panel_weight,
    near_list,
    far_list,
    far_class,
    far_count,
    coarse_list,
    coarse_class,
    coarse_count,
    couple_fine,
    couple_coarse,
    up_transfer,
    down_transfer,
):
    own = jnp.concatenate(
        [krylov_block, points, panel_size[None], panel_weight[None], jnp.zeros((3, W), F32)], axis=0
    )
    up = [(i, i + 1) for i in range(D - 1)]
    down = [(i + 1, i) for i in range(D - 1)]
    left = lax.ppermute(own, BOX, up)
    right = lax.ppermute(own, BOX, down)
    sent = call(poles_kernel, sds(D, 7, 128), 2, 7, name="poles")(
        far_count, coarse_count, krylov_block, bases, up_transfer, far_list, far_class, coarse_list, coarse_class
    )
    got = exchange(sent, BOX)
    coarse_all = exchange(call(coarse_send_kernel, sds(16, 16, 128), 0, 1, name="coarse_send")(got), LEAF)
    fine = call(
        fine_kernel,
        sds(C * D, 64),
        0,
        2,
        [pltpu.VMEM((FAR1, C * D, 128), F32), pltpu.VMEM((FAR1, C * D, 128), F32)],
        name="fine",
    )(got, couple_fine)
    near = call(
        near_kernel,
        sds(Q, W),
        1,
        3,
        [
            pltpu.VMEM((3 * C, 4, M, M), F32),
            pltpu.VMEM((3 * C, Q, M), BF16),
            pltpu.VMEM((3 * C, Q, M), BF16),
        ],
        name="near",
    )(near_list, left, own, right)
    back = call(coarse_kernel, sds(D, 4, 128), 0, 5, name="coarse")(
        got, coarse_all, couple_coarse, down_transfer, fine
    )
    local = exchange(back, BOX)
    product, grams = call(product_kernel, (sds(Q, W), sds(D, 3, 128)), 0, 4, name="product")(
        local, near, krylov_block, bases
    )
    part = jnp.sum(exchange(grams, PLANE), axis=0)
    part = exchange(jnp.broadcast_to(part[None], (16, 3, 128)), "box_0")
    part = jnp.sum(part, axis=0)
    whole = exchange(jnp.broadcast_to(part[None], (D, 3, 128)), PLANE)
    return call(finish_kernel, (sds(Q, W), sds(Q, Q), sds(Q, Q)), 0, 3, name="finish")(
        whole, krylov_block, product
    )


def solution(mesh):
    split = Mesh(mesh.devices.reshape(4, 4, 16, 2), LEAF_BOX)
    placed = (
        P(None, LEAF_BOX),
        P(None, LEAF_BOX),
        P(None, LEAF_BOX),
        P(LEAF_BOX),
        P(LEAF_BOX),
        P(LEAF_BOX, None),
        P(LEAF_BOX, None),
        P(LEAF_BOX, None),
        P(LEAF_BOX),
        P(LEAF_BOX, None),
        P(LEAF_BOX, None),
        P(LEAF_BOX),
        P(),
        P(),
        P(),
        P(),
    )
    return jax.shard_map(
        per_device,
        mesh=split,
        in_specs=placed,
        out_specs=(P(None, LEAF_BOX), P(), P()),
        check_vma=False,
    )
```

```python
import jax
import jax.numpy as jnp
from jax import lax
from jax.experimental import pallas as pl
from jax.experimental.pallas import tpu as pltpu
from jax.sharding import Mesh
from jax.sharding import PartitionSpec as P

LEAF = ("leaf_0", "leaf_1")
BOX = ("box_0", "box_1")
LEAF_BOX = LEAF + BOX
PLANE = ("leaf_0", "leaf_1", "box_1")
F32 = jnp.float32
BF16 = jnp.bfloat16
HI = lax.Precision.HIGHEST
NT = (((1,), (1,)), ((), ()))
TN = (((0,), (0,)), ((), ()))

Q = 64
R = 32
M = 128
C = 8
NEAR = 16
FAR1 = 12
FAR2 = 16
D = 32
W = C * M


def nn(a, b):
    return jnp.dot(a, b, precision=HI, preferred_element_type=F32)


def nt(a, b):
    return lax.dot_general(a, b, NT, precision=HI, preferred_element_type=F32)


def tn(a, b):
    return lax.dot_general(a, b, TN, precision=HI, preferred_element_type=F32)


def bdot(a, b):
    return jnp.dot(a, b, preferred_element_type=F32)


def halves(x):
    hi = x.astype(BF16)
    return hi, (x - hi.astype(F32)).astype(BF16)


def dense(ref, buf):
    for k in range(buf.shape[0]):
        buf[k] = ref[:, k, :]
    return [buf[k] for k in range(buf.shape[0])]


def lane_flat(x, rows, width):
    wide = jnp.concatenate([x] * rows + [jnp.zeros((rows, 128 - rows * width), F32)], axis=1)
    lane = lax.broadcasted_iota(jnp.int32, (rows, 128), 1)
    row = lax.broadcasted_iota(jnp.int32, (rows, 128), 0)
    keep = (lane >= row * width) & (lane < (row + 1) * width)
    return jnp.sum(jnp.where(keep, wide, 0.0), axis=0, keepdims=True)


def poles_kernel(*refs):
    sources = refs[:9]
    out_ref = refs[9]
    copies = [pltpu.make_async_copy(a, b, refs[19].at[k]) for k, (a, b) in enumerate(zip(sources, refs[10:19]))]
    for copy in copies:
        copy.start()
    for copy in copies:
        copy.wait()
    far_count, coarse_count, v_ref, b_ref, up_ref, far_list, far_class, coarse_list, coarse_class = refs[10:19]
    parts = []
    coarse = jnp.zeros((Q, R), F32)
    for b in range(C):
        cols = slice(b * M, (b + 1) * M)
        pole = nt(v_ref[:, cols], b_ref[:, cols])
        coarse = coarse + nn(pole, up_ref[b])
        parts.append(pole)
    for half in range(2):
        rows = slice(half * D, (half + 1) * D)
        for t in range(2):
            out_ref[:, 2 * half + t, :] = jnp.concatenate([p[rows] for p in parts[4 * t : 4 * t + 4]], axis=1)
    slot = lax.broadcasted_iota(jnp.int32, (C, FAR1), 1)
    row = lax.broadcasted_iota(jnp.int32, (C, FAR1), 0)
    live = jnp.zeros((C, FAR1), jnp.int32)
    for b in range(C):
        live = jnp.where(row == b, far_count[b], live)
    box = far_list[...] & 255
    place = ((box & 7) * D + (box >> 3)).astype(F32)
    place = jnp.where(slot < live, place, -1.0)
    out_ref[:, 5, :] = jnp.broadcast_to(lane_flat(place, C, FAR1), (D, 128))
    out_ref[:, 6, :] = jnp.broadcast_to(lane_flat(far_class[...].astype(F32), C, FAR1), (D, 128))
    parent = coarse_list[...]
    inner = parent & 31
    spot = ((parent >> 5) * 16 + (inner & 15) + (inner >> 4) * 256).astype(F32)
    spot = jnp.where(lax.broadcasted_iota(jnp.int32, (1, FAR2), 1) < coarse_count[0], spot, -1.0)
    tail = jnp.concatenate(
        [spot, coarse_class[...].astype(F32), jnp.zeros((1, 128 - 64 - 2 * FAR2), F32)], axis=1
    )
    out_ref[:, 4, :] = jnp.concatenate(
        [coarse[:D], coarse[D:], jnp.broadcast_to(tail, (D, 64))], axis=1
    )


def near_kernel(index, left, own, right, out_ref, geo, vhi, vlo):
    for part, ref in enumerate((left, own, right)):
        for s in range(C):
            cols = slice(s * M, (s + 1) * M)
            turned = jnp.transpose(ref[Q : Q + 8, cols])
            for k in range(4):
                geo[part * C + s, k] = jnp.broadcast_to(turned[:, k : k + 1], (M, M))
            value = ref[:Q, cols] * (ref[Q + 4 : Q + 5, cols] * (1.0 / (M * NEAR)))
            hi, lo = halves(value)
            vhi[part * C + s] = hi
            vlo[part * C + s] = lo
    base = index[0, 0] - C

    def one_box(b, carry):
        cols = pl.ds(pl.multiple_of(b * M, M), M)
        target = [own[Q + k : Q + k + 1, cols] for k in range(4)]
        acc = jnp.zeros((Q, M), F32)
        for pair in range(NEAR // 2):
            ghi = []
            glo = []
            at = [index[b, 2 * pair + k] - base for k in range(2)]
            for i in at:
                d0 = geo[i, 0] - target[0]
                d1 = geo[i, 1] - target[1]
                d2 = geo[i, 2] - target[2]
                g = lax.rsqrt(d0 * d0 + d1 * d1 + d2 * d2 + geo[i, 3] * target[3])
                hi, lo = halves(g)
                ghi.append(hi)
                glo.append(lo)
            ghi = jnp.concatenate(ghi, axis=0)
            glo = jnp.concatenate(glo, axis=0)
            xhi = jnp.concatenate([vhi[i] for i in at], axis=1)
            xlo = jnp.concatenate([vlo[i] for i in at], axis=1)
            acc = acc + bdot(xhi, ghi) + (bdot(xlo, ghi) + bdot(xhi, glo))
        out_ref[:, cols] = acc
        return carry

    lax.fori_loop(0, C, one_box, 0)


def coarse_send_kernel(got_ref, out_ref, buf):
    buf[...] = got_ref[:, 4, :]
    pole = buf[...]
    both = jnp.concatenate([pole[:16, :64], pole[16:, :64]], axis=1)
    for k in range(16):
        out_ref[k] = both


def doubled(x):
    return x + pltpu.roll(x, 64, 1)


def tables_kernel(fine, coarse, down, fine_out, coarse_out, down_out):
    zero = jnp.zeros((R, R), F32)
    for table, out in ((fine, fine_out), (coarse, coarse_out)):
        for u in range(4):
            top = []
            low = []
            for k in range(4):
                top += [table[4 * u + k], zero]
                low += [zero, table[4 * u + k]]
            hi, lo = halves(jnp.concatenate([jnp.concatenate(top, axis=1), jnp.concatenate(low, axis=1)], axis=0))
            out[u] = jnp.concatenate([hi, lo], axis=0)
    rows = [jnp.concatenate([down[j], zero], axis=1) for j in range(C)]
    rows += [jnp.concatenate([zero, down[j]], axis=1) for j in range(C)]
    hi, lo = halves(jnp.concatenate(rows, axis=0))
    down_out[0] = hi
    down_out[1] = lo


def bnt(a, b):
    return lax.dot_general(a, b, NT, preferred_element_type=F32)


def fine_kernel(got_ref, table, out_ref, zhi, zlo, buf):
    got = dense(got_ref, buf)
    pieces = []
    for j in range(C):
        lanes = slice((j % 4) * R, (j % 4 + 1) * R)
        pieces.append(jnp.concatenate([got[j // 4][:, lanes], got[2 + j // 4][:, lanes]], axis=1))
    hi, lo = halves(jnp.concatenate(pieces, axis=0))
    source = jnp.concatenate([hi, lo], axis=1)
    place = got[5]
    kind = got[6]
    lane = lax.broadcasted_iota(jnp.int32, (D, C * D), 1).astype(F32)
    odd = (lax.broadcasted_iota(jnp.int32, (D, 128), 1) >= 64).astype(F32)
    for j in range(C):
        hot = []
        for e in range(FAR1):
            k = j * FAR1 + e
            hot.append(jnp.where(jnp.broadcast_to(place[:, k : k + 1], (D, C * D)) == lane, 1.0, 0.0))
        picked = doubled(bdot(jnp.concatenate(hot, axis=0).astype(BF16), source))
        z = [jnp.zeros((D, 128), F32) for t in range(8)]
        for e in range(FAR1):
            k = j * FAR1 + e
            which = jnp.broadcast_to(kind[:, k : k + 1], (D, 128)) - odd
            term = picked[e * D : (e + 1) * D]
            for t in range(8):
                z[t] = z[t] + jnp.where(which == 2.0 * t, term, 0.0)
        for t in range(8):
            hi, lo = halves(z[t])
            zhi[t // 2, j * D : (j + 1) * D, (t % 2) * 128 : (t % 2 + 1) * 128] = hi
            zlo[t // 2, j * D : (j + 1) * D, (t % 2) * 128 : (t % 2 + 1) * 128] = lo
    total = jnp.zeros((C * D, 128), F32)
    extra = jnp.zeros((C * D, 64), F32)
    for u in range(4):
        total = total + bnt(zhi[u], table[u])
        extra = extra + bnt(zlo[u], table[u, :64])
    total = total[:, :64] + total[:, 64:] + extra
    for q in range(2):
        for h in range(2):
            out_ref[2 * q + h] = jnp.concatenate(
                [total[(4 * h + k) * D : (4 * h + k + 1) * D, q * R : (q + 1) * R] for k in range(4)], axis=1
            )


def coarse_kernel(got_ref, all_ref, table, down, fine_ref, out_ref, buf):
    hi, lo = halves(all_ref[...].reshape(256, 128))
    source = jnp.concatenate(
        [
            jnp.concatenate([hi[:, :64], lo[:, :64]], axis=1),
            jnp.concatenate([hi[:, 64:], lo[:, 64:]], axis=1),
        ],
        axis=0,
    )
    buf[...] = got_ref[:, 4, :]
    listed = buf[...]
    lane = lax.broadcasted_iota(jnp.int32, (D, 512), 1).astype(F32)
    hot = [
        jnp.where(jnp.broadcast_to(listed[:, 64 + e : 65 + e], (D, 512)) == lane, 1.0, 0.0)
        for e in range(FAR2)
    ]
    picked = doubled(bdot(jnp.concatenate(hot, axis=0).astype(BF16), source))
    odd = (lax.broadcasted_iota(jnp.int32, (D, 128), 1) >= 64).astype(F32)
    z = [jnp.zeros((D, 128), F32) for t in range(8)]
    for e in range(FAR2):
        which = jnp.broadcast_to(listed[:, 64 + FAR2 + e : 65 + FAR2 + e], (D, 128)) - odd
        term = picked[e * D : (e + 1) * D]
        for t in range(8):
            z[t] = z[t] + jnp.where(which == 2.0 * t, term, 0.0)
    total = jnp.zeros((2 * D, 128), F32)
    for u in range(4):
        hi, lo = halves(jnp.concatenate(z[2 * u : 2 * u + 2], axis=1))
        total = total + bnt(jnp.concatenate([hi, lo], axis=0), table[u])
    hi, lo = halves(total[:D, :64] + total[:D, 64:] + total[D:, :64])
    spread = bnt(hi, down[0]) + (bnt(lo, down[0]) + bnt(hi, down[1]))
    for t in range(4):
        out_ref[:, t, :] = fine_ref[t] + spread[:, t * 128 : (t + 1) * 128]


def product_kernel(got_ref, near_ref, v_ref, b_ref, out_ref, gram_ref, buf):
    got = dense(got_ref, buf)
    for b in range(C):
        cols = slice(b * M, (b + 1) * M)
        lanes = slice((b % 4) * R, (b % 4 + 1) * R)
        local = jnp.concatenate([got[b // 4][:, lanes], got[2 + b // 4][:, lanes]], axis=0)
        out_ref[:, cols] = near_ref[:, cols] + nn(local, b_ref[:, cols])
    v = v_ref[...]
    image = out_ref[...]
    for k, g in enumerate((nt(v, v), nt(v, image), nt(image, image))):
        gram_ref[:, k, :] = jnp.concatenate([g[:D], g[D:]], axis=1)


def finish_kernel(got_ref, v_ref, p_ref, next_ref, hess_ref, factor_ref, buf):
    panels = float(M * C * D * 16)
    basis, mixed, image = [jnp.concatenate([g[:, :64], g[:, 64:]], axis=0) for g in dense(got_ref, buf)]
    hess = mixed * (1.0 / panels)
    hess_ref[...] = hess
    cross = tn(mixed, hess)
    gram = (image - cross - jnp.transpose(cross) + nn(tn(hess, basis), hess)) * (1.0 / panels)
    residual = p_ref[...] - tn(hess, v_ref[...])
    row = lax.broadcasted_iota(jnp.int32, (Q, Q), 0)
    col = lax.broadcasted_iota(jnp.int32, (Q, Q), 1)
    work = jnp.concatenate([gram, jnp.where(row == col, 1.0, 0.0)], axis=1)
    tiles = [work[8 * k : 8 * k + 8] for k in range(8)]
    sub = lax.broadcasted_iota(jnp.int32, (8, 128), 0)
    scales = [jnp.zeros((8, 128), F32) for k in range(8)]
    for j in range(0, Q, 2):
        own = j // 8
        at = j % 8
        tile = tiles[own]
        first = jnp.broadcast_to(tile[:, j : j + 1], (8, 128))
        second = jnp.broadcast_to(tile[:, j + 1 : j + 2], (8, 128))
        corner = jnp.broadcast_to(first[at : at + 1], (8, 128))
        below = jnp.broadcast_to(first[at + 1 : at + 2], (8, 128))
        right = jnp.broadcast_to(second[at : at + 1], (8, 128))
        line = jnp.broadcast_to(tile[at : at + 1], (8, 128))
        inverse = 1.0 / corner
        ratio = below * inverse
        across = right * inverse
        pivot = jnp.broadcast_to(second[at + 1 : at + 2], (8, 128)) - ratio * right
        following = jnp.broadcast_to(tile[at + 1 : at + 2], (8, 128)) - ratio * line
        line = line * inverse
        scaled = following * (1.0 / pivot)
        scales[own] = jnp.where(sub == at, corner, jnp.where(sub == at + 1, pivot, scales[own]))
        if at < 6:
            lower = tile - first * line - (second - first * across) * scaled
            tiles[own] = jnp.where(sub > at + 1, lower, jnp.where(sub == at + 1, following, tile))
        else:
            tiles[own] = jnp.where(sub == at + 1, following, tile)
        for k in range(own + 1, 8):
            first = jnp.broadcast_to(tiles[k][:, j : j + 1], (8, 128))
            second = jnp.broadcast_to(tiles[k][:, j + 1 : j + 2], (8, 128))
            tiles[k] = tiles[k] - first * line - (second - first * across) * scaled
    whole = jnp.concatenate([tiles[k] * lax.rsqrt(scales[k]) for k in range(8)], axis=0)
    factor_ref[...] = jnp.transpose(jnp.where(col >= row, whole[:, :Q], 0.0))
    next_ref[...] = nn(whole[:, Q:], residual)


def sds(*shape):
    return jax.ShapeDtypeStruct(shape, F32)


def bds(*shape):
    return jax.ShapeDtypeStruct(shape, BF16)


SMEM = pl.BlockSpec(memory_space=pltpu.SMEM)
VMEM = pl.BlockSpec(memory_space=pltpu.VMEM)


def call(kernel, out, smem=0, vmem=0, scratch=(), name=None):
    return pl.pallas_call(
        kernel,
        out_shape=out,
        in_specs=[SMEM] * smem + [VMEM] * vmem,
        out_specs=jax.tree.map(lambda _: VMEM, out),
        scratch_shapes=list(scratch),
        compiler_params=pltpu.CompilerParams(vmem_limit_bytes=48 << 20),
        name=name,
    )


def exchange(blocks, axes):
    return lax.all_to_all(blocks, axes, 0, 0, tiled=True)


def per_device(
    krylov_block,
    bases,
    points,
    panel_size,
    panel_weight,
    near_list,
    far_list,
    far_class,
    far_count,
    coarse_list,
    coarse_class,
    coarse_count,
    couple_fine,
    couple_coarse,
    up_transfer,
    down_transfer,
):
    own = jnp.concatenate(
        [krylov_block, points, panel_size[None], panel_weight[None], jnp.zeros((3, W), F32)], axis=0
    )
    up = [(i, i + 1) for i in range(D - 1)]
    down = [(i + 1, i) for i in range(D - 1)]
    left = lax.ppermute(own, BOX, up)
    right = lax.ppermute(own, BOX, down)
    sent = pl.pallas_call(
        poles_kernel,
        out_shape=sds(D, 7, 128),
        in_specs=[pl.BlockSpec(memory_space=pltpu.HBM)] * 9,
        out_specs=VMEM,
        scratch_shapes=[
            pltpu.SMEM((C,), jnp.int32),
            pltpu.SMEM((1,), jnp.int32),
            pltpu.VMEM((Q, W), F32),
            pltpu.VMEM((R, W), F32),
            pltpu.VMEM((C, R, R), F32),
            pltpu.VMEM((C, FAR1), jnp.int32),
            pltpu.VMEM((C, FAR1), jnp.int32),
            pltpu.VMEM((1, FAR2), jnp.int32),
            pltpu.VMEM((1, FAR2), jnp.int32),
            pltpu.SemaphoreType.DMA((9,)),
        ],
        name="poles",
    )(far_count, coarse_count, krylov_block, bases, up_transfer, far_list, far_class, coarse_list, coarse_class)
    got = exchange(sent, BOX)
    fine_table, coarse_table, down_table = call(
        tables_kernel, (bds(4, 128, 256), bds(4, 128, 256), bds(2, 2 * C * R, 2 * R)), 0, 3, name="tables"
    )(couple_fine, couple_coarse, down_transfer)
    got, left, right, fine_table, coarse_table, down_table = lax.optimization_barrier(
        (got, left, right, fine_table, coarse_table, down_table)
    )
    coarse_all = exchange(call(
        coarse_send_kernel, sds(16, 16, 128), 0, 1, [pltpu.VMEM((D, 128), F32)], name="coarse_send"
    )(got), LEAF)
    fine = call(
        fine_kernel,
        sds(4, D, 128),
        0,
        2,
        [pltpu.VMEM((4, C * D, 256), BF16), pltpu.VMEM((4, C * D, 256), BF16), pltpu.VMEM((7, D, 128), F32)],
        name="fine",
    )(got, fine_table)
    near = call(
        near_kernel,
        sds(Q, W),
        1,
        3,
        [
            pltpu.VMEM((3 * C, 4, M, M), F32),
            pltpu.VMEM((3 * C, Q, M), BF16),
            pltpu.VMEM((3 * C, Q, M), BF16),
        ],
        name="near",
    )(near_list, left, own, right)
    back = call(coarse_kernel, sds(D, 4, 128), 0, 5, [pltpu.VMEM((D, 128), F32)], name="coarse")(
        got, coarse_all, coarse_table, down_table, fine
    )
    local = exchange(back, BOX)
    product, grams = call(product_kernel, (sds(Q, W), sds(D, 3, 128)), 0, 4, [pltpu.VMEM((4, D, 128), F32)], name="product")(
        local, near, krylov_block, bases
    )
    part = jnp.sum(exchange(grams, PLANE), axis=0)
    part = exchange(jnp.broadcast_to(part[None], (16, 3, 128)), "box_0")
    part = jnp.sum(part, axis=0)
    whole = exchange(jnp.broadcast_to(part[None], (D, 3, 128)), PLANE)
    return call(finish_kernel, (sds(Q, W), sds(Q, Q), sds(Q, Q)), 0, 3, [pltpu.VMEM((3, D, 128), F32)], name="finish")(
        whole, krylov_block, product
    )


def solution(mesh):
    split = Mesh(mesh.devices.reshape(4, 4, 16, 2), LEAF_BOX)
    placed = (
        P(None, LEAF_BOX),
        P(None, LEAF_BOX),
        P(None, LEAF_BOX),
        P(LEAF_BOX),
        P(LEAF_BOX),
        P(LEAF_BOX, None),
        P(LEAF_BOX, None),
        P(LEAF_BOX, None),
        P(LEAF_BOX),
        P(LEAF_BOX, None),
        P(LEAF_BOX, None),
        P(LEAF_BOX),
        P(),
        P(),
        P(),
        P(),
    )
    return jax.shard_map(
        per_device,
        mesh=split,
        in_specs=placed,
        out_specs=(P(None, LEAF_BOX), P(), P()),
        check_vma=False,
    )
```

```python
import jax
import jax.numpy as jnp
from jax import lax
from jax.experimental import pallas as pl
from jax.experimental.pallas import tpu as pltpu
from jax.sharding import Mesh
from jax.sharding import PartitionSpec as P

LEAF = ("leaf_0", "leaf_1")
BOX = ("box_0", "box_1")
LEAF_BOX = LEAF + BOX
PLANE = ("leaf_0", "leaf_1", "box_1")
F32 = jnp.float32
BF16 = jnp.bfloat16
HI = lax.Precision.HIGHEST
NT = (((1,), (1,)), ((), ()))
TN = (((0,), (0,)), ((), ()))

Q = 64
R = 32
M = 128
C = 8
NEAR = 16
FAR1 = 12
FAR2 = 16
D = 32
W = C * M


def nn(a, b):
    return jnp.dot(a, b, precision=HI, preferred_element_type=F32)


def nt(a, b):
    return lax.dot_general(a, b, NT, precision=HI, preferred_element_type=F32)


def tn(a, b):
    return lax.dot_general(a, b, TN, precision=HI, preferred_element_type=F32)


def bdot(a, b):
    return jnp.dot(a, b, preferred_element_type=F32)


def halves(x):
    hi = x.astype(BF16)
    return hi, (x - hi.astype(F32)).astype(BF16)


def dense(ref, buf):
    for k in range(buf.shape[0]):
        buf[k] = ref[:, k, :]
    return [buf[k] for k in range(buf.shape[0])]


def lane_flat(x, rows, width):
    wide = jnp.concatenate([x] * rows + [jnp.zeros((rows, 128 - rows * width), F32)], axis=1)
    lane = lax.broadcasted_iota(jnp.int32, (rows, 128), 1)
    row = lax.broadcasted_iota(jnp.int32, (rows, 128), 0)
    keep = (lane >= row * width) & (lane < (row + 1) * width)
    return jnp.sum(jnp.where(keep, wide, 0.0), axis=0, keepdims=True)


def poles_kernel(*refs):
    sources = refs[:12]
    out_ref, own = refs[12:14]
    own[Q : Q + 8, :] = jnp.zeros((8, W), F32)
    places = list(refs[14:16]) + [own.at[pl.ds(0, Q)]] + list(refs[16:22])
    places += [own.at[pl.ds(Q, 3)], own.at[pl.ds(Q + 3, 1)], own.at[pl.ds(Q + 4, 1)]]
    copies = [pltpu.make_async_copy(x, y, refs[22].at[k]) for k, (x, y) in enumerate(zip(sources, places))]
    for copy in copies:
        copy.start()
    for copy in copies:
        copy.wait()
    far_count, coarse_count, b_ref, up_ref, far_list, far_class, coarse_list, coarse_class = refs[14:22]
    v_ref = own
    parts = []
    coarse = jnp.zeros((Q, R), F32)
    for b in range(C):
        cols = slice(b * M, (b + 1) * M)
        pole = nt(v_ref[:Q, cols], b_ref[:, cols])
        coarse = coarse + nn(pole, up_ref[b])
        parts.append(pole)
    for half in range(2):
        rows = slice(half * D, (half + 1) * D)
        for t in range(2):
            out_ref[:, 2 * half + t, :] = jnp.concatenate([p[rows] for p in parts[4 * t : 4 * t + 4]], axis=1)
    slot = lax.broadcasted_iota(jnp.int32, (C, FAR1), 1)
    row = lax.broadcasted_iota(jnp.int32, (C, FAR1), 0)
    live = jnp.zeros((C, FAR1), jnp.int32)
    for b in range(C):
        live = jnp.where(row == b, far_count[b], live)
    box = far_list[...] & 255
    place = ((box & 7) * D + (box >> 3)).astype(F32)
    place = jnp.where(slot < live, place, -1.0)
    out_ref[:, 5, :] = jnp.broadcast_to(lane_flat(place, C, FAR1), (D, 128))
    out_ref[:, 6, :] = jnp.broadcast_to(lane_flat(far_class[...].astype(F32), C, FAR1), (D, 128))
    parent = coarse_list[...]
    inner = parent & 31
    spot = ((parent >> 5) * 16 + (inner & 15) + (inner >> 4) * 256).astype(F32)
    spot = jnp.where(lax.broadcasted_iota(jnp.int32, (1, FAR2), 1) < coarse_count[0], spot, -1.0)
    tail = jnp.concatenate(
        [spot, coarse_class[...].astype(F32), jnp.zeros((1, 128 - 64 - 2 * FAR2), F32)], axis=1
    )
    out_ref[:, 4, :] = jnp.concatenate(
        [coarse[:D], coarse[D:], jnp.broadcast_to(tail, (D, 64))], axis=1
    )


def bnt(a, b):
    return lax.dot_general(a, b, NT, preferred_element_type=F32)


def near_kernel(index, left, own, right, out_ref, geo, vhi, vlo, rows):
    for part, ref in enumerate((left, own, right)):
        for s in range(C):
            cols = slice(s * M, (s + 1) * M)
            rows[part * C + s] = ref[Q : Q + 4, cols]
            value = ref[:Q, cols] * (ref[Q + 4 : Q + 5, cols] * (1.0 / (M * NEAR)))
            hi, lo = halves(value)
            vhi[part * C + s] = hi
            vlo[part * C + s] = lo
    for s in range(C):
        turned = jnp.transpose(own[Q : Q + 8, s * M : (s + 1) * M])
        for k in range(4):
            geo[s, k] = jnp.broadcast_to(turned[:, k : k + 1], (M, M))
    base = index[0, 0] - C

    def one_box(b, carry):
        acc = jnp.zeros((Q, M), F32)
        for pair in range(NEAR // 2):
            ghi = []
            glo = []
            at = [index[b, 2 * pair + k] - base for k in range(2)]
            for i in at:
                d0 = geo[b, 0] - rows[i, 0:1]
                d1 = geo[b, 1] - rows[i, 1:2]
                d2 = geo[b, 2] - rows[i, 2:3]
                g = lax.rsqrt(d0 * d0 + d1 * d1 + d2 * d2 + geo[b, 3] * rows[i, 3:4])
                hi, lo = halves(g)
                ghi.append(hi)
                glo.append(lo)
            ghi = jnp.concatenate(ghi, axis=1)
            glo = jnp.concatenate(glo, axis=1)
            xhi = jnp.concatenate([vhi[i] for i in at], axis=1)
            xlo = jnp.concatenate([vlo[i] for i in at], axis=1)
            both = bnt(jnp.concatenate([xhi, xlo], axis=0), ghi)
            acc = acc + (both[:Q] + (both[Q:] + bnt(xhi, glo)))
        out_ref[:, pl.ds(pl.multiple_of(b * M, M), M)] = acc
        return carry

    lax.fori_loop(0, C, one_box, 0)


def coarse_send_kernel(got_ref, out_ref, buf):
    buf[...] = got_ref[:, 4, :]
    pole = buf[...]
    both = jnp.concatenate([pole[:16, :64], pole[16:, :64]], axis=1)
    for k in range(16):
        out_ref[k] = both


def doubled(x):
    return x + pltpu.roll(x, 64, 1)


def tables_kernel(fine, coarse, down, fine_out, coarse_out, down_out):
    zero = jnp.zeros((R, R), F32)
    for table, out in ((fine, fine_out), (coarse, coarse_out)):
        for u in range(4):
            top = []
            low = []
            for k in range(4):
                top += [table[4 * u + k], zero]
                low += [zero, table[4 * u + k]]
            hi, lo = halves(jnp.concatenate([jnp.concatenate(top, axis=1), jnp.concatenate(low, axis=1)], axis=0))
            out[u] = jnp.concatenate([hi, lo], axis=0)
    rows = [jnp.concatenate([down[j], zero], axis=1) for j in range(C)]
    rows += [jnp.concatenate([zero, down[j]], axis=1) for j in range(C)]
    hi, lo = halves(jnp.concatenate(rows, axis=0))
    down_out[0] = hi
    down_out[1] = lo


def fine_kernel(got_ref, table, out_ref, zhi, zlo, buf):
    got = dense(got_ref, buf)
    pieces = []
    for j in range(C):
        lanes = slice((j % 4) * R, (j % 4 + 1) * R)
        pieces.append(jnp.concatenate([got[j // 4][:, lanes], got[2 + j // 4][:, lanes]], axis=1))
    hi, lo = halves(jnp.concatenate(pieces, axis=0))
    source = jnp.concatenate([hi, lo], axis=1)
    place = got[5]
    kind = got[6]
    lane = lax.broadcasted_iota(jnp.int32, (D, C * D), 1).astype(F32)
    odd = (lax.broadcasted_iota(jnp.int32, (D, 128), 1) >= 64).astype(F32)
    for j in range(C):
        hot = []
        for e in range(FAR1):
            k = j * FAR1 + e
            hot.append(jnp.where(jnp.broadcast_to(place[:, k : k + 1], (D, C * D)) == lane, 1.0, 0.0))
        picked = doubled(bdot(jnp.concatenate(hot, axis=0).astype(BF16), source))
        z = [jnp.zeros((D, 128), F32) for t in range(8)]
        for e in range(FAR1):
            k = j * FAR1 + e
            which = jnp.broadcast_to(kind[:, k : k + 1], (D, 128)) - odd
            term = picked[e * D : (e + 1) * D]
            for t in range(8):
                z[t] = z[t] + jnp.where(which == 2.0 * t, term, 0.0)
        for t in range(8):
            hi, lo = halves(z[t])
            zhi[t // 2, j * D : (j + 1) * D, (t % 2) * 128 : (t % 2 + 1) * 128] = hi
            zlo[t // 2, j * D : (j + 1) * D, (t % 2) * 128 : (t % 2 + 1) * 128] = lo
    total = jnp.zeros((C * D, 128), F32)
    extra = jnp.zeros((C * D, 64), F32)
    for u in range(4):
        total = total + bnt(zhi[u], table[u])
        extra = extra + bnt(zlo[u], table[u, :64])
    total = total[:, :64] + total[:, 64:] + extra
    for q in range(2):
        for h in range(2):
            out_ref[2 * q + h] = jnp.concatenate(
                [total[(4 * h + k) * D : (4 * h + k + 1) * D, q * R : (q + 1) * R] for k in range(4)], axis=1
            )


def coarse_kernel(got_ref, all_ref, table, down, fine_ref, out_ref, buf):
    hi, lo = halves(all_ref[...].reshape(256, 128))
    source = jnp.concatenate(
        [
            jnp.concatenate([hi[:, :64], lo[:, :64]], axis=1),
            jnp.concatenate([hi[:, 64:], lo[:, 64:]], axis=1),
        ],
        axis=0,
    )
    buf[...] = got_ref[:, 4, :]
    listed = buf[...]
    lane = lax.broadcasted_iota(jnp.int32, (D, 512), 1).astype(F32)
    hot = [
        jnp.where(jnp.broadcast_to(listed[:, 64 + e : 65 + e], (D, 512)) == lane, 1.0, 0.0)
        for e in range(FAR2)
    ]
    picked = doubled(bdot(jnp.concatenate(hot, axis=0).astype(BF16), source))
    odd = (lax.broadcasted_iota(jnp.int32, (D, 128), 1) >= 64).astype(F32)
    z = [jnp.zeros((D, 128), F32) for t in range(8)]
    for e in range(FAR2):
        which = jnp.broadcast_to(listed[:, 64 + FAR2 + e : 65 + FAR2 + e], (D, 128)) - odd
        term = picked[e * D : (e + 1) * D]
        for t in range(8):
            z[t] = z[t] + jnp.where(which == 2.0 * t, term, 0.0)
    total = jnp.zeros((2 * D, 128), F32)
    for u in range(4):
        hi, lo = halves(jnp.concatenate(z[2 * u : 2 * u + 2], axis=1))
        total = total + bnt(jnp.concatenate([hi, lo], axis=0), table[u])
    hi, lo = halves(total[:D, :64] + total[:D, 64:] + total[D:, :64])
    spread = bnt(hi, down[0]) + (bnt(lo, down[0]) + bnt(hi, down[1]))
    for t in range(4):
        out_ref[:, t, :] = fine_ref[t] + spread[:, t * 128 : (t + 1) * 128]


def product_kernel(got_ref, near_ref, v_ref, b_ref, out_ref, gram_ref, buf):
    got = dense(got_ref, buf)
    for b in range(C):
        cols = slice(b * M, (b + 1) * M)
        lanes = slice((b % 4) * R, (b % 4 + 1) * R)
        local = jnp.concatenate([got[b // 4][:, lanes], got[2 + b // 4][:, lanes]], axis=0)
        out_ref[:, cols] = near_ref[:, cols] + nn(local, b_ref[:, cols])
    v = v_ref[...]
    image = out_ref[...]
    for k, g in enumerate((nt(v, v), nt(v, image), nt(image, image))):
        gram_ref[:, k, :] = jnp.concatenate([g[:D], g[D:]], axis=1)


def row_of(x, mask):
    return jnp.broadcast_to(jnp.sum(jnp.where(mask, x, 0.0), axis=0, keepdims=True), (8, 128))


def finish_kernel(got_ref, v_ref, p_ref, next_ref, hess_ref, factor_ref, buf):
    panels = float(M * C * D * 16)
    basis, mixed, image = [jnp.concatenate([g[:, :64], g[:, 64:]], axis=0) for g in dense(got_ref, buf)]
    hess = mixed * (1.0 / panels)
    hess_ref[...] = hess
    cross = tn(mixed, hess)
    gram = (image - cross - jnp.transpose(cross) + nn(tn(hess, basis), hess)) * (1.0 / panels)
    residual = p_ref[...] - tn(hess, v_ref[...])
    row = lax.broadcasted_iota(jnp.int32, (Q, Q), 0)
    col = lax.broadcasted_iota(jnp.int32, (Q, Q), 1)
    work = jnp.concatenate([gram, jnp.where(row == col, 1.0, 0.0)], axis=1)
    tiles = [work[8 * k : 8 * k + 8] for k in range(8)]
    sub = lax.broadcasted_iota(jnp.int32, (8, 128), 0)
    scales = [jnp.zeros((8, 128), F32) for k in range(8)]
    for j in range(0, Q, 2):
        own = j // 8
        at = j % 8
        tile = tiles[own]
        first = jnp.broadcast_to(tile[:, j : j + 1], (8, 128))
        second = jnp.broadcast_to(tile[:, j + 1 : j + 2], (8, 128))
        line = jnp.broadcast_to(tile[at : at + 1], (8, 128))
        following = jnp.broadcast_to(tile[at + 1 : at + 2], (8, 128))
        corner = row_of(first, sub == at)
        right = row_of(second, sub == at)
        below = row_of(first, sub == at + 1)
        pivot = row_of(second, sub == at + 1)
        inverse = 1.0 / corner
        ratio = below * inverse
        across = right * inverse
        pivot = pivot - ratio * right
        following = following - ratio * line
        line = line * inverse
        scaled = following * (1.0 / pivot)
        scales[own] = jnp.where(sub == at, corner, jnp.where(sub == at + 1, pivot, scales[own]))
        if at < 6:
            lower = tile - first * line - (second - first * across) * scaled
            tiles[own] = jnp.where(sub > at + 1, lower, jnp.where(sub == at + 1, following, tile))
        else:
            tiles[own] = jnp.where(sub == at + 1, following, tile)
        for k in range(own + 1, 8):
            first = jnp.broadcast_to(tiles[k][:, j : j + 1], (8, 128))
            second = jnp.broadcast_to(tiles[k][:, j + 1 : j + 2], (8, 128))
            tiles[k] = tiles[k] - first * line - (second - first * across) * scaled
    whole = jnp.concatenate([tiles[k] * lax.rsqrt(scales[k]) for k in range(8)], axis=0)
    factor_ref[...] = jnp.transpose(jnp.where(col >= row, whole[:, :Q], 0.0))
    next_ref[...] = nn(whole[:, Q:], residual)


def sds(*shape):
    return jax.ShapeDtypeStruct(shape, F32)


def bds(*shape):
    return jax.ShapeDtypeStruct(shape, BF16)


SMEM = pl.BlockSpec(memory_space=pltpu.SMEM)
VMEM = pl.BlockSpec(memory_space=pltpu.VMEM)


def call(kernel, out, smem=0, vmem=0, scratch=(), name=None):
    return pl.pallas_call(
        kernel,
        out_shape=out,
        in_specs=[SMEM] * smem + [VMEM] * vmem,
        out_specs=jax.tree.map(lambda _: VMEM, out),
        scratch_shapes=list(scratch),
        compiler_params=pltpu.CompilerParams(vmem_limit_bytes=48 << 20),
        name=name,
    )


def exchange(blocks, axes):
    return lax.all_to_all(blocks, axes, 0, 0, tiled=True)


def per_device(
    krylov_block,
    bases,
    points,
    panel_size,
    panel_weight,
    near_list,
    far_list,
    far_class,
    far_count,
    coarse_list,
    coarse_class,
    coarse_count,
    couple_fine,
    couple_coarse,
    up_transfer,
    down_transfer,
):
    up = [(i, i + 1) for i in range(D - 1)]
    down = [(i + 1, i) for i in range(D - 1)]
    sent, own = pl.pallas_call(
        poles_kernel,
        out_shape=(sds(D, 7, 128), sds(Q + 8, W)),
        in_specs=[pl.BlockSpec(memory_space=pltpu.HBM)] * 12,
        out_specs=(VMEM, VMEM),
        scratch_shapes=[
            pltpu.SMEM((C,), jnp.int32),
            pltpu.SMEM((1,), jnp.int32),
            pltpu.VMEM((R, W), F32),
            pltpu.VMEM((C, R, R), F32),
            pltpu.VMEM((C, FAR1), jnp.int32),
            pltpu.VMEM((C, FAR1), jnp.int32),
            pltpu.VMEM((1, FAR2), jnp.int32),
            pltpu.VMEM((1, FAR2), jnp.int32),
            pltpu.SemaphoreType.DMA((12,)),
        ],
        name="poles",
    )(
        far_count,
        coarse_count,
        krylov_block,
        bases,
        up_transfer,
        far_list,
        far_class,
        coarse_list,
        coarse_class,
        points,
        panel_size[None],
        panel_weight[None],
    )
    left = lax.ppermute(own, BOX, up)
    right = lax.ppermute(own, BOX, down)
    got = exchange(sent, BOX)
    fine_table, coarse_table, down_table = call(
        tables_kernel, (bds(4, 128, 256), bds(4, 128, 256), bds(2, 2 * C * R, 2 * R)), 0, 3, name="tables"
    )(couple_fine, couple_coarse, down_transfer)
    got, left, right, fine_table, coarse_table, down_table = lax.optimization_barrier(
        (got, left, right, fine_table, coarse_table, down_table)
    )
    coarse_all = exchange(call(
        coarse_send_kernel, sds(16, 16, 128), 0, 1, [pltpu.VMEM((D, 128), F32)], name="coarse_send"
    )(got), LEAF)
    fine = call(
        fine_kernel,
        sds(4, D, 128),
        0,
        2,
        [pltpu.VMEM((4, C * D, 256), BF16), pltpu.VMEM((4, C * D, 256), BF16), pltpu.VMEM((7, D, 128), F32)],
        name="fine",
    )(got, fine_table)
    near = call(
        near_kernel,
        sds(Q, W),
        1,
        3,
        [
            pltpu.VMEM((C, 4, M, M), F32),
            pltpu.VMEM((3 * C, Q, M), BF16),
            pltpu.VMEM((3 * C, Q, M), BF16),
            pltpu.VMEM((3 * C, 4, M), F32),
        ],
        name="near",
    )(near_list, left, own, right)
    back = call(coarse_kernel, sds(D, 4, 128), 0, 5, [pltpu.VMEM((D, 128), F32)], name="coarse")(
        got, coarse_all, coarse_table, down_table, fine
    )
    local = exchange(back, BOX)
    product, grams = call(product_kernel, (sds(Q, W), sds(D, 3, 128)), 0, 4, [pltpu.VMEM((4, D, 128), F32)], name="product")(
        local, near, krylov_block, bases
    )
    part = jnp.sum(exchange(grams, PLANE), axis=0)
    part = exchange(jnp.broadcast_to(part[None], (16, 3, 128)), "box_0")
    part = jnp.sum(part, axis=0)
    whole = exchange(jnp.broadcast_to(part[None], (D, 3, 128)), PLANE)
    return call(finish_kernel, (sds(Q, W), sds(Q, Q), sds(Q, Q)), 0, 3, [pltpu.VMEM((3, D, 128), F32)], name="finish")(
        whole, krylov_block, product
    )


def solution(mesh):
    split = Mesh(mesh.devices.reshape(4, 4, 16, 2), LEAF_BOX)
    placed = (
        P(None, LEAF_BOX),
        P(None, LEAF_BOX),
        P(None, LEAF_BOX),
        P(LEAF_BOX),
        P(LEAF_BOX),
        P(LEAF_BOX, None),
        P(LEAF_BOX, None),
        P(LEAF_BOX, None),
        P(LEAF_BOX),
        P(LEAF_BOX, None),
        P(LEAF_BOX, None),
        P(LEAF_BOX),
        P(),
        P(),
        P(),
        P(),
    )
    return jax.shard_map(
        per_device,
        mesh=split,
        in_specs=placed,
        out_specs=(P(None, LEAF_BOX), P(), P()),
        check_vma=False,
    )
```

```python
import jax
import jax.numpy as jnp
from jax import lax
from jax.experimental import pallas as pl
from jax.experimental.pallas import tpu as pltpu
from jax.sharding import Mesh
from jax.sharding import PartitionSpec as P

LEAF = ("leaf_0", "leaf_1")
BOX = ("box_0", "box_1")
LEAF_BOX = LEAF + BOX
PLANE = ("leaf_0", "leaf_1", "box_1")
F32 = jnp.float32
BF16 = jnp.bfloat16
HI = lax.Precision.HIGHEST
NT = (((1,), (1,)), ((), ()))
TN = (((0,), (0,)), ((), ()))

Q = 64
R = 32
M = 128
C = 8
NEAR = 16
FAR1 = 12
FAR2 = 16
D = 32
W = C * M


def nn(a, b):
    return jnp.dot(a, b, precision=HI, preferred_element_type=F32)


def nt(a, b):
    return lax.dot_general(a, b, NT, precision=HI, preferred_element_type=F32)


def tn(a, b):
    return lax.dot_general(a, b, TN, precision=HI, preferred_element_type=F32)


def bdot(a, b):
    return jnp.dot(a, b, preferred_element_type=F32)


def halves(x):
    hi = x.astype(BF16)
    return hi, (x - hi.astype(F32)).astype(BF16)


def dense(ref, buf):
    for k in range(buf.shape[0]):
        buf[k] = ref[:, k, :]
    return [buf[k] for k in range(buf.shape[0])]


def lane_flat(x, rows, width):
    wide = jnp.concatenate([x] * rows + [jnp.zeros((rows, 128 - rows * width), F32)], axis=1)
    lane = lax.broadcasted_iota(jnp.int32, (rows, 128), 1)
    row = lax.broadcasted_iota(jnp.int32, (rows, 128), 0)
    keep = (lane >= row * width) & (lane < (row + 1) * width)
    return jnp.sum(jnp.where(keep, wide, 0.0), axis=0, keepdims=True)


def poles_kernel(*refs):
    sources = refs[:12]
    out_ref, own = refs[12:14]
    own[Q : Q + 8, :] = jnp.zeros((8, W), F32)
    places = list(refs[14:16]) + [own.at[pl.ds(0, Q)]] + list(refs[16:22])
    places += [own.at[pl.ds(Q, 3)], own.at[pl.ds(Q + 3, 1)], own.at[pl.ds(Q + 4, 1)]]
    copies = [pltpu.make_async_copy(x, y, refs[22].at[k]) for k, (x, y) in enumerate(zip(sources, places))]
    for copy in copies:
        copy.start()
    for copy in copies:
        copy.wait()
    far_count, coarse_count, b_ref, up_ref, far_list, far_class, coarse_list, coarse_class = refs[14:22]
    v_ref = own
    parts = []
    coarse = jnp.zeros((Q, R), F32)
    for b in range(C):
        cols = slice(b * M, (b + 1) * M)
        pole = nt(v_ref[:Q, cols], b_ref[:, cols])
        coarse = coarse + nn(pole, up_ref[b])
        parts.append(pole)
    for half in range(2):
        rows = slice(half * D, (half + 1) * D)
        for t in range(2):
            out_ref[:, 2 * half + t, :] = jnp.concatenate([p[rows] for p in parts[4 * t : 4 * t + 4]], axis=1)
    slot = lax.broadcasted_iota(jnp.int32, (C, FAR1), 1)
    row = lax.broadcasted_iota(jnp.int32, (C, FAR1), 0)
    live = jnp.zeros((C, FAR1), jnp.int32)
    for b in range(C):
        live = jnp.where(row == b, far_count[b], live)
    box = far_list[...] & 255
    place = ((box & 7) * D + (box >> 3)).astype(F32)
    place = jnp.where(slot < live, place, -1.0)
    out_ref[:, 5, :] = jnp.broadcast_to(lane_flat(place, C, FAR1), (D, 128))
    out_ref[:, 6, :] = jnp.broadcast_to(lane_flat(far_class[...].astype(F32), C, FAR1), (D, 128))
    parent = coarse_list[...]
    inner = parent & 31
    spot = ((parent >> 5) * 16 + (inner & 15) + (inner >> 4) * 256).astype(F32)
    spot = jnp.where(lax.broadcasted_iota(jnp.int32, (1, FAR2), 1) < coarse_count[0], spot, -1.0)
    tail = jnp.concatenate(
        [spot, coarse_class[...].astype(F32), jnp.zeros((1, 128 - 64 - 2 * FAR2), F32)], axis=1
    )
    out_ref[:, 4, :] = jnp.concatenate(
        [coarse[:D], coarse[D:], jnp.broadcast_to(tail, (D, 64))], axis=1
    )


def bnt(a, b):
    return lax.dot_general(a, b, NT, preferred_element_type=F32)


def spread(out, columns):
    for k in range(4):
        out[k] = jnp.broadcast_to(columns[:, k : k + 1], (M, M))


def near_kernel(listed, inner, own, outer, out_ref, index, sem, turned, even, odd, vhi, vlo, rows):
    copy = pltpu.make_async_copy(listed, index, sem)
    copy.start()
    for part, ref in enumerate((inner, own, outer)):
        for s in range(C):
            cols = slice(s * M, (s + 1) * M)
            rows[part * C + s] = ref[Q : Q + 4, cols]
            value = ref[:Q, cols] * (ref[Q + 4 : Q + 5, cols] * (1.0 / (M * NEAR)))
            hi, lo = halves(value)
            vhi[part * C + s] = hi
            vlo[part * C + s] = lo
    for s in range(C):
        turned[s] = jnp.transpose(own[Q : Q + 8, s * M : (s + 1) * M])
    spread(even, turned[0])
    copy.wait()
    base = index[0, 0] - C
    flip = 16 * (1 - ((index[0, 0] >> 3) & 1))

    def one_box(b, geo, ahead):
        acc = jnp.zeros((Q, M), F32)
        for pair in range(NEAR // 2):
            ghi = []
            glo = []
            at = [index[b, 2 * pair + k] - base for k in range(2)]
            at = [i + flip * (1 - (i >> 3)) for i in at]
            for i in at:
                d0 = geo[0] - rows[i, 0:1]
                d1 = geo[1] - rows[i, 1:2]
                d2 = geo[2] - rows[i, 2:3]
                g = lax.rsqrt(d0 * d0 + d1 * d1 + d2 * d2 + geo[3] * rows[i, 3:4])
                hi, lo = halves(g)
                ghi.append(hi)
                glo.append(lo)
            ghi = jnp.concatenate(ghi, axis=1)
            glo = jnp.concatenate(glo, axis=1)
            xhi = jnp.concatenate([vhi[i] for i in at], axis=1)
            xlo = jnp.concatenate([vlo[i] for i in at], axis=1)
            both = bnt(jnp.concatenate([xhi, xlo], axis=0), ghi)
            acc = acc + (both[:Q] + (both[Q:] + bnt(xhi, glo)))
        out_ref[:, pl.ds(pl.multiple_of(b * M, M), M)] = acc
        spread(ahead, turned[(b + 1) & 7])

    def two_boxes(i, carry):
        one_box(2 * i, even, odd)
        one_box(2 * i + 1, odd, even)
        return carry

    lax.fori_loop(0, C // 2, two_boxes, 0)


def coarse_send_kernel(got_ref, out_ref, buf):
    buf[...] = got_ref[:, 4, :]
    pole = buf[...]
    both = jnp.concatenate([pole[:16, :64], pole[16:, :64]], axis=1)
    for k in range(16):
        out_ref[k] = both


def doubled(x):
    return x + pltpu.roll(x, 64, 1)


def tables_kernel(fine, coarse, down, fine_out, coarse_out, down_out):
    zero = jnp.zeros((R, R), F32)
    for table, out in ((fine, fine_out), (coarse, coarse_out)):
        for u in range(4):
            top = []
            low = []
            for k in range(4):
                top += [table[4 * u + k], zero]
                low += [zero, table[4 * u + k]]
            hi, lo = halves(jnp.concatenate([jnp.concatenate(top, axis=1), jnp.concatenate(low, axis=1)], axis=0))
            out[u] = jnp.concatenate([hi, lo], axis=0)
    rows = [jnp.concatenate([down[j], zero], axis=1) for j in range(C)]
    rows += [jnp.concatenate([zero, down[j]], axis=1) for j in range(C)]
    hi, lo = halves(jnp.concatenate(rows, axis=0))
    down_out[0] = hi
    down_out[1] = lo


def fine_kernel(got_ref, table, out_ref, zhi, zlo, buf):
    got = dense(got_ref, buf)
    pieces = []
    for j in range(C):
        lanes = slice((j % 4) * R, (j % 4 + 1) * R)
        pieces.append(jnp.concatenate([got[j // 4][:, lanes], got[2 + j // 4][:, lanes]], axis=1))
    hi, lo = halves(jnp.concatenate(pieces, axis=0))
    source = jnp.concatenate([hi, lo], axis=1)
    place = got[5]
    kind = got[6]
    lane = lax.broadcasted_iota(jnp.int32, (D, C * D), 1).astype(F32)
    odd = (lax.broadcasted_iota(jnp.int32, (D, 128), 1) >= 64).astype(F32)
    for j in range(C):
        hot = []
        for e in range(FAR1):
            k = j * FAR1 + e
            hot.append(jnp.where(jnp.broadcast_to(place[:, k : k + 1], (D, C * D)) == lane, 1.0, 0.0))
        picked = doubled(bdot(jnp.concatenate(hot, axis=0).astype(BF16), source))
        z = [jnp.zeros((D, 128), F32) for _ in range(8)]
        for e in range(FAR1):
            k = j * FAR1 + e
            which = jnp.broadcast_to(kind[:, k : k + 1], (D, 128)) - odd
            term = picked[e * D : (e + 1) * D]
            for t in range(8):
                z[t] = z[t] + jnp.where(which == 2.0 * t, term, 0.0)
        for t in range(8):
            hi, lo = halves(z[t])
            zhi[t // 2, j * D : (j + 1) * D, (t % 2) * 128 : (t % 2 + 1) * 128] = hi
            zlo[t // 2, j * D : (j + 1) * D, (t % 2) * 128 : (t % 2 + 1) * 128] = lo
    total = jnp.zeros((C * D, 128), F32)
    extra = jnp.zeros((C * D, 64), F32)
    for u in range(4):
        total = total + bnt(zhi[u], table[u])
        extra = extra + bnt(zlo[u], table[u, :64])
    total = total[:, :64] + total[:, 64:] + extra
    for q in range(2):
        for h in range(2):
            out_ref[2 * q + h] = jnp.concatenate(
                [total[(4 * h + k) * D : (4 * h + k + 1) * D, q * R : (q + 1) * R] for k in range(4)], axis=1
            )


def coarse_kernel(got_ref, all_ref, table, down, fine_ref, out_ref, buf):
    hi, lo = halves(all_ref[...].reshape(256, 128))
    source = jnp.concatenate(
        [
            jnp.concatenate([hi[:, :64], lo[:, :64]], axis=1),
            jnp.concatenate([hi[:, 64:], lo[:, 64:]], axis=1),
        ],
        axis=0,
    )
    buf[...] = got_ref[:, 4, :]
    listed = buf[...]
    lane = lax.broadcasted_iota(jnp.int32, (D, 512), 1).astype(F32)
    hot = [
        jnp.where(jnp.broadcast_to(listed[:, 64 + e : 65 + e], (D, 512)) == lane, 1.0, 0.0)
        for e in range(FAR2)
    ]
    picked = doubled(bdot(jnp.concatenate(hot, axis=0).astype(BF16), source))
    odd = (lax.broadcasted_iota(jnp.int32, (D, 128), 1) >= 64).astype(F32)
    z = [jnp.zeros((D, 128), F32) for _ in range(8)]
    for e in range(FAR2):
        which = jnp.broadcast_to(listed[:, 64 + FAR2 + e : 65 + FAR2 + e], (D, 128)) - odd
        term = picked[e * D : (e + 1) * D]
        for t in range(8):
            z[t] = z[t] + jnp.where(which == 2.0 * t, term, 0.0)
    total = jnp.zeros((2 * D, 128), F32)
    for u in range(4):
        hi, lo = halves(jnp.concatenate(z[2 * u : 2 * u + 2], axis=1))
        total = total + bnt(jnp.concatenate([hi, lo], axis=0), table[u])
    hi, lo = halves(total[:D, :64] + total[:D, 64:] + total[D:, :64])
    spread = bnt(hi, down[0]) + (bnt(lo, down[0]) + bnt(hi, down[1]))
    for t in range(4):
        out_ref[:, t, :] = fine_ref[t] + spread[:, t * 128 : (t + 1) * 128]


def product_kernel(got_ref, near_ref, v_ref, b_ref, out_ref, gram_ref, buf):
    got = dense(got_ref, buf)
    for b in range(C):
        cols = slice(b * M, (b + 1) * M)
        lanes = slice((b % 4) * R, (b % 4 + 1) * R)
        local = jnp.concatenate([got[b // 4][:, lanes], got[2 + b // 4][:, lanes]], axis=0)
        out_ref[:, cols] = near_ref[:, cols] + nn(local, b_ref[:, cols])
    v = v_ref[...]
    image = out_ref[...]
    for k, g in enumerate((nt(v, v), nt(v, image), nt(image, image))):
        gram_ref[:, k, :] = jnp.concatenate([g[:D], g[D:]], axis=1)


def row_of(x, mask):
    return jnp.broadcast_to(jnp.sum(jnp.where(mask, x, 0.0), axis=0, keepdims=True), (8, 128))


def finish_kernel(got_ref, v_ref, p_ref, next_ref, hess_ref, factor_ref, buf):
    panels = float(M * C * D * 16)
    basis, mixed, image = [jnp.concatenate([g[:, :64], g[:, 64:]], axis=0) for g in dense(got_ref, buf)]
    hess = mixed * (1.0 / panels)
    hess_ref[...] = hess
    cross = tn(mixed, hess)
    gram = (image - cross - jnp.transpose(cross) + nn(tn(hess, basis), hess)) * (1.0 / panels)
    residual = p_ref[...] - tn(hess, v_ref[...])
    row = lax.broadcasted_iota(jnp.int32, (Q, Q), 0)
    col = lax.broadcasted_iota(jnp.int32, (Q, Q), 1)
    work = jnp.concatenate([gram, jnp.where(row == col, 1.0, 0.0)], axis=1)
    tiles = [work[8 * k : 8 * k + 8] for k in range(8)]
    sub = lax.broadcasted_iota(jnp.int32, (8, 128), 0)
    scales = [jnp.zeros((8, 128), F32) for _ in range(8)]
    for j in range(0, Q, 2):
        own = j // 8
        at = j % 8
        tile = tiles[own]
        first = jnp.broadcast_to(tile[:, j : j + 1], (8, 128))
        second = jnp.broadcast_to(tile[:, j + 1 : j + 2], (8, 128))
        line = jnp.broadcast_to(tile[at : at + 1], (8, 128))
        following = jnp.broadcast_to(tile[at + 1 : at + 2], (8, 128))
        corner = row_of(first, sub == at)
        right = row_of(second, sub == at)
        below = row_of(first, sub == at + 1)
        pivot = row_of(second, sub == at + 1)
        inverse = 1.0 / corner
        ratio = below * inverse
        across = right * inverse
        pivot = pivot - ratio * right
        following = following - ratio * line
        line = line * inverse
        scaled = following * (1.0 / pivot)
        scales[own] = jnp.where(sub == at, corner, jnp.where(sub == at + 1, pivot, scales[own]))
        if at < 6:
            lower = tile - first * line - (second - first * across) * scaled
            tiles[own] = jnp.where(sub > at + 1, lower, jnp.where(sub == at + 1, following, tile))
        else:
            tiles[own] = jnp.where(sub == at + 1, following, tile)
        for k in range(own + 1, 8):
            first = jnp.broadcast_to(tiles[k][:, j : j + 1], (8, 128))
            second = jnp.broadcast_to(tiles[k][:, j + 1 : j + 2], (8, 128))
            tiles[k] = tiles[k] - first * line - (second - first * across) * scaled
    whole = jnp.concatenate([tiles[k] * lax.rsqrt(scales[k]) for k in range(8)], axis=0)
    factor_ref[...] = jnp.transpose(jnp.where(col >= row, whole[:, :Q], 0.0))
    next_ref[...] = nn(whole[:, Q:], residual)


def sds(*shape):
    return jax.ShapeDtypeStruct(shape, F32)


def bds(*shape):
    return jax.ShapeDtypeStruct(shape, BF16)


SMEM = pl.BlockSpec(memory_space=pltpu.SMEM)
VMEM = pl.BlockSpec(memory_space=pltpu.VMEM)


def call(kernel, out, smem=0, vmem=0, scratch=()):
    return pl.pallas_call(
        kernel,
        out_shape=out,
        in_specs=[SMEM] * smem + [VMEM] * vmem,
        out_specs=jax.tree.map(lambda _: VMEM, out),
        scratch_shapes=list(scratch),
        compiler_params=pltpu.CompilerParams(vmem_limit_bytes=16 << 20),
    )


def exchange(blocks, axes):
    return lax.all_to_all(blocks, axes, 0, 0, tiled=True)


def step(
    krylov_block,
    bases,
    points,
    panel_size,
    panel_weight,
    near_list,
    far_list,
    far_class,
    far_count,
    coarse_list,
    coarse_class,
    coarse_count,
    couple_fine,
    couple_coarse,
    up_transfer,
    down_transfer,
):
    sent, own = pl.pallas_call(
        poles_kernel,
        out_shape=(sds(D, 7, 128), sds(Q + 8, W)),
        in_specs=[pl.BlockSpec(memory_space=pltpu.HBM)] * 12,
        out_specs=(VMEM, VMEM),
        scratch_shapes=[
            pltpu.SMEM((C,), jnp.int32),
            pltpu.SMEM((1,), jnp.int32),
            pltpu.VMEM((R, W), F32),
            pltpu.VMEM((C, R, R), F32),
            pltpu.VMEM((C, FAR1), jnp.int32),
            pltpu.VMEM((C, FAR1), jnp.int32),
            pltpu.VMEM((1, FAR2), jnp.int32),
            pltpu.VMEM((1, FAR2), jnp.int32),
            pltpu.SemaphoreType.DMA((12,)),
        ],
        name="poles",
    )(
        far_count,
        coarse_count,
        krylov_block,
        bases,
        up_transfer,
        far_list,
        far_class,
        coarse_list,
        coarse_class,
        points,
        panel_size[None],
        panel_weight[None],
    )
    inner = lax.ppermute(own, BOX, [(i, i ^ 1) for i in range(D)])
    outer = lax.ppermute(own, BOX, [(i, ((i + 1) ^ 1) - 1) for i in range(1, D - 1)])
    got = exchange(sent, BOX)
    fine_table, coarse_table, down_table = call(
        tables_kernel, (bds(4, 128, 256), bds(4, 128, 256), bds(2, 2 * C * R, 2 * R)), 0, 3
    )(couple_fine, couple_coarse, down_transfer)
    near = pl.pallas_call(
        near_kernel,
        out_shape=sds(Q, W),
        in_specs=[pl.BlockSpec(memory_space=pltpu.HBM)] + [VMEM] * 3,
        out_specs=VMEM,
        scratch_shapes=[
            pltpu.SMEM((C, NEAR), jnp.int32),
            pltpu.SemaphoreType.DMA,
            pltpu.VMEM((C, M, 8), F32),
            pltpu.VMEM((4, M, M), F32),
            pltpu.VMEM((4, M, M), F32),
            pltpu.VMEM((3 * C, Q, M), BF16),
            pltpu.VMEM((3 * C, Q, M), BF16),
            pltpu.VMEM((3 * C, 4, M), F32),
        ],
        compiler_params=pltpu.CompilerParams(vmem_limit_bytes=16 << 20),
        name="near",
    )(near_list, inner, own, outer)
    got, near, fine_table, coarse_table, down_table = lax.optimization_barrier(
        (got, near, fine_table, coarse_table, down_table)
    )
    coarse_all = exchange(call(coarse_send_kernel, sds(16, 16, 128), 0, 1, [pltpu.VMEM((D, 128), F32)])(got), LEAF)
    fine = call(
        fine_kernel,
        sds(4, D, 128),
        0,
        2,
        [pltpu.VMEM((4, C * D, 256), BF16), pltpu.VMEM((4, C * D, 256), BF16), pltpu.VMEM((7, D, 128), F32)],
    )(got, fine_table)
    back = call(coarse_kernel, sds(D, 4, 128), 0, 5, [pltpu.VMEM((D, 128), F32)])(
        got, coarse_all, coarse_table, down_table, fine
    )
    local = exchange(back, BOX)
    product, grams = call(product_kernel, (sds(Q, W), sds(D, 3, 128)), 0, 4, [pltpu.VMEM((4, D, 128), F32)])(
        local, near, krylov_block, bases
    )
    part = jnp.sum(exchange(grams, PLANE), axis=0)
    part = exchange(jnp.broadcast_to(part[None], (16, 3, 128)), "box_0")
    part = jnp.sum(part, axis=0)
    whole = exchange(jnp.broadcast_to(part[None], (D, 3, 128)), PLANE)
    return call(finish_kernel, (sds(Q, W), sds(Q, Q), sds(Q, Q)), 0, 3, [pltpu.VMEM((3, D, 128), F32)])(
        whole, krylov_block, product
    )


def solution(mesh):
    split = Mesh(mesh.devices.reshape(4, 4, 16, 2), LEAF_BOX)
    placed = (
        P(None, LEAF_BOX),
        P(None, LEAF_BOX),
        P(None, LEAF_BOX),
        P(LEAF_BOX),
        P(LEAF_BOX),
        P(LEAF_BOX, None),
        P(LEAF_BOX, None),
        P(LEAF_BOX, None),
        P(LEAF_BOX),
        P(LEAF_BOX, None),
        P(LEAF_BOX, None),
        P(LEAF_BOX),
        P(),
        P(),
        P(),
        P(),
    )
    return jax.shard_map(
        step,
        mesh=split,
        in_specs=placed,
        out_specs=(P(None, LEAF_BOX), P(), P()),
        check_vma=False,
    )
```

```python
import jax
import jax.numpy as jnp
from jax import lax
from jax.experimental import pallas as pl
from jax.experimental.pallas import tpu as pltpu
from jax.sharding import Mesh
from jax.sharding import PartitionSpec as P

LEAF = ("leaf_0", "leaf_1")
BOX = ("box_0", "box_1")
LEAF_BOX = LEAF + BOX
PLANE = ("leaf_0", "leaf_1", "box_1")
F32 = jnp.float32
BF16 = jnp.bfloat16
HI = lax.Precision.HIGHEST
NT = (((1,), (1,)), ((), ()))
TN = (((0,), (0,)), ((), ()))

Q = 64
R = 32
M = 128
C = 8
NEAR = 16
FAR1 = 12
FAR2 = 16
D = 32
W = C * M


def nn(a, b):
    return jnp.dot(a, b, precision=HI, preferred_element_type=F32)


def nt(a, b):
    return lax.dot_general(a, b, NT, precision=HI, preferred_element_type=F32)


def tn(a, b):
    return lax.dot_general(a, b, TN, precision=HI, preferred_element_type=F32)


def bdot(a, b):
    return jnp.dot(a, b, preferred_element_type=F32)


def bnt(a, b):
    return lax.dot_general(a, b, NT, preferred_element_type=F32)


def halves(x):
    hi = x.astype(BF16)
    return hi, (x - hi.astype(F32)).astype(BF16)


def dense(ref, buf):
    for k in range(buf.shape[0]):
        buf[k] = ref[:, 0, k * 128 : (k + 1) * 128]
    return [buf[k] for k in range(buf.shape[0])]


def lane_flat(x, rows, width):
    wide = jnp.concatenate([x] * rows + [jnp.zeros((rows, 128 - rows * width), F32)], axis=1)
    lane = lax.broadcasted_iota(jnp.int32, (rows, 128), 1)
    row = lax.broadcasted_iota(jnp.int32, (rows, 128), 0)
    keep = (lane >= row * width) & (lane < (row + 1) * width)
    return jnp.sum(jnp.where(keep, wide, 0.0), axis=0, keepdims=True)


def poles_kernel(*refs):
    sources = refs[:12]
    out_ref, own = refs[12:14]
    own[Q : Q + 8, :] = jnp.zeros((8, W), F32)
    places = list(refs[14:16]) + [own.at[pl.ds(0, Q)]] + list(refs[16:22])
    places += [own.at[pl.ds(Q, 3)], own.at[pl.ds(Q + 3, 1)], own.at[pl.ds(Q + 4, 1)]]
    copies = [pltpu.make_async_copy(x, y, refs[22].at[k]) for k, (x, y) in enumerate(zip(sources, places))]
    for copy in copies:
        copy.start()
    for copy in copies:
        copy.wait()
    far_count, coarse_count, b_ref, up_ref, far_list, far_class, coarse_list, coarse_class = refs[14:22]
    v_ref = own
    parts = []
    coarse = jnp.zeros((Q, R), F32)
    for b in range(C):
        cols = slice(b * M, (b + 1) * M)
        vhi, vlo = halves(v_ref[:Q, cols])
        bhi, blo = halves(b_ref[:, cols])
        both = bnt(jnp.concatenate([vhi, vlo], axis=0), bhi)
        pole = both[:Q] + (both[Q:] + bnt(vhi, blo))
        parts.append(pole)
    for b in range(C):
        phi, plo = halves(parts[b])
        uhi, ulo = halves(up_ref[b])
        both = bdot(jnp.concatenate([phi, plo], axis=0), uhi)
        coarse = coarse + (both[:Q] + (both[Q:] + bdot(phi, ulo)))
    for half in range(2):
        rows = slice(half * D, (half + 1) * D)
        for t in range(2):
            out_ref[:, 0, (2 * half + t) * 128 : (2 * half + t + 1) * 128] = jnp.concatenate([p[rows] for p in parts[4 * t : 4 * t + 4]], axis=1)
    slot = lax.broadcasted_iota(jnp.int32, (C, FAR1), 1)
    row = lax.broadcasted_iota(jnp.int32, (C, FAR1), 0)
    live = jnp.zeros((C, FAR1), jnp.int32)
    for b in range(C):
        live = jnp.where(row == b, far_count[b], live)
    box = far_list[...] & 255
    place = ((box & 7) * D + (box >> 3)).astype(F32)
    place = jnp.where(slot < live, place, -1.0)
    out_ref[:, 0, 640:768] = jnp.broadcast_to(lane_flat(place, C, FAR1), (D, 128))
    out_ref[:, 0, 768:896] = jnp.broadcast_to(lane_flat(far_class[...].astype(F32), C, FAR1), (D, 128))
    parent = coarse_list[...]
    inner = parent & 31
    spot = ((parent >> 5) * 16 + (inner & 15) + (inner >> 4) * 256).astype(F32)
    spot = jnp.where(lax.broadcasted_iota(jnp.int32, (1, FAR2), 1) < coarse_count[0], spot, -1.0)
    tail = jnp.concatenate(
        [spot, coarse_class[...].astype(F32), jnp.zeros((1, 128 - 64 - 2 * FAR2), F32)], axis=1
    )
    out_ref[:, 0, 512:640] = jnp.concatenate(
        [coarse[:D], coarse[D:], jnp.broadcast_to(tail, (D, 64))], axis=1
    )


def spread(out, columns):
    for k in range(4):
        out[k] = jnp.broadcast_to(columns[:, k : k + 1], (M, M))


def near_kernel(listed, inner, own, outer, out_ref, index, sem, turned, even, odd, vhi, vlo, rows):
    copy = pltpu.make_async_copy(listed, index, sem)
    copy.start()
    for part, ref in enumerate((inner, own, outer)):
        for s in range(C):
            cols = slice(s * M, (s + 1) * M)
            rows[part * C + s] = ref[Q : Q + 4, cols]
            value = ref[:Q, cols] * (ref[Q + 4 : Q + 5, cols] * (1.0 / (M * NEAR)))
            hi, lo = halves(value)
            vhi[part * C + s] = hi
            vlo[part * C + s] = lo
    for s in range(C):
        turned[s] = jnp.transpose(own[Q : Q + 8, s * M : (s + 1) * M])
    spread(even, turned[0])
    copy.wait()
    base = index[0, 0] - C
    flip = 16 * (1 - ((index[0, 0] >> 3) & 1))

    def one_box(b, geo, ahead):
        acc = jnp.zeros((Q, M), F32)
        for pair in range(NEAR // 2):
            ghi = []
            glo = []
            at = [index[b, 2 * pair + k] - base for k in range(2)]
            at = [i + flip * (1 - (i >> 3)) for i in at]
            for i in at:
                d0 = geo[0] - rows[i, 0:1]
                d1 = geo[1] - rows[i, 1:2]
                d2 = geo[2] - rows[i, 2:3]
                g = lax.rsqrt(d0 * d0 + d1 * d1 + d2 * d2 + geo[3] * rows[i, 3:4])
                hi, lo = halves(g)
                ghi.append(hi)
                glo.append(lo)
            ghi = jnp.concatenate(ghi, axis=1)
            glo = jnp.concatenate(glo, axis=1)
            xhi = jnp.concatenate([vhi[i] for i in at], axis=1)
            xlo = jnp.concatenate([vlo[i] for i in at], axis=1)
            both = bnt(jnp.concatenate([xhi, xlo], axis=0), ghi)
            acc = acc + (both[:Q] + (both[Q:] + bnt(xhi, glo)))
        out_ref[:, pl.ds(pl.multiple_of(b * M, M), M)] = acc
        spread(ahead, turned[(b + 1) & 7])

    def two_boxes(i, carry):
        one_box(2 * i, even, odd)
        one_box(2 * i + 1, odd, even)
        return carry

    lax.fori_loop(0, C // 2, two_boxes, 0)


def coarse_send_kernel(got_ref, out_ref, buf):
    buf[...] = got_ref[:, 0, 512:640]
    pole = buf[...]
    both = jnp.concatenate([pole[:16, :64], pole[16:, :64]], axis=1)
    for k in range(16):
        out_ref[k] = both


def doubled(x):
    return x + pltpu.roll(x, 64, 1)


def tables_kernel(fine, coarse, down, fine_out, coarse_out, down_out):
    zero = jnp.zeros((R, R), F32)
    for table, out in ((fine, fine_out), (coarse, coarse_out)):
        for u in range(4):
            top = []
            low = []
            for k in range(4):
                top += [table[4 * u + k], zero]
                low += [zero, table[4 * u + k]]
            hi, lo = halves(jnp.concatenate([jnp.concatenate(top, axis=1), jnp.concatenate(low, axis=1)], axis=0))
            out[u] = jnp.concatenate([hi, lo], axis=0)
    rows = [jnp.concatenate([down[j], zero], axis=1) for j in range(C)]
    rows += [jnp.concatenate([zero, down[j]], axis=1) for j in range(C)]
    hi, lo = halves(jnp.concatenate(rows, axis=0))
    down_out[0] = hi
    down_out[1] = lo


def fine_kernel(got_ref, table, out_ref, zhi, zlo, buf):
    got = dense(got_ref, buf)
    pieces = []
    for j in range(C):
        lanes = slice((j % 4) * R, (j % 4 + 1) * R)
        pieces.append(jnp.concatenate([got[j // 4][:, lanes], got[2 + j // 4][:, lanes]], axis=1))
    hi, lo = halves(jnp.concatenate(pieces, axis=0))
    source = jnp.concatenate([hi, lo], axis=1)
    place = got[5]
    kind = got[6]
    lane = lax.broadcasted_iota(jnp.int32, (D, C * D), 1).astype(F32)
    odd = (lax.broadcasted_iota(jnp.int32, (D, 128), 1) >= 64).astype(F32)
    for j in range(C):
        hot = []
        for e in range(FAR1):
            k = j * FAR1 + e
            hot.append(jnp.where(jnp.broadcast_to(place[:, k : k + 1], (D, C * D)) == lane, 1.0, 0.0))
        picked = doubled(bdot(jnp.concatenate(hot, axis=0).astype(BF16), source))
        z = [jnp.zeros((D, 128), F32) for _ in range(8)]
        for e in range(FAR1):
            k = j * FAR1 + e
            which = jnp.broadcast_to(kind[:, k : k + 1], (D, 128)) - odd
            term = picked[e * D : (e + 1) * D]
            for t in range(8):
                z[t] = z[t] + jnp.where(which == 2.0 * t, term, 0.0)
        for t in range(8):
            hi, lo = halves(z[t])
            zhi[t // 2, j * D : (j + 1) * D, (t % 2) * 128 : (t % 2 + 1) * 128] = hi
            zlo[t // 2, j * D : (j + 1) * D, (t % 2) * 128 : (t % 2 + 1) * 128] = lo
    total = jnp.zeros((C * D, 128), F32)
    extra = jnp.zeros((C * D, 64), F32)
    for u in range(4):
        total = total + bnt(zhi[u], table[u])
        extra = extra + bnt(zlo[u], table[u, :64])
    total = total[:, :64] + total[:, 64:] + extra
    for q in range(2):
        for h in range(2):
            out_ref[2 * q + h] = jnp.concatenate(
                [total[(4 * h + k) * D : (4 * h + k + 1) * D, q * R : (q + 1) * R] for k in range(4)], axis=1
            )


def coarse_kernel(got_ref, all_ref, table, down, fine_ref, out_ref, buf):
    hi, lo = halves(all_ref[...].reshape(256, 128))
    source = jnp.concatenate(
        [
            jnp.concatenate([hi[:, :64], lo[:, :64]], axis=1),
            jnp.concatenate([hi[:, 64:], lo[:, 64:]], axis=1),
        ],
        axis=0,
    )
    buf[...] = got_ref[:, 0, 512:640]
    listed = buf[...]
    lane = lax.broadcasted_iota(jnp.int32, (D, 512), 1).astype(F32)
    hot = [
        jnp.where(jnp.broadcast_to(listed[:, 64 + e : 65 + e], (D, 512)) == lane, 1.0, 0.0)
        for e in range(FAR2)
    ]
    picked = doubled(bdot(jnp.concatenate(hot, axis=0).astype(BF16), source))
    odd = (lax.broadcasted_iota(jnp.int32, (D, 128), 1) >= 64).astype(F32)
    z = [jnp.zeros((D, 128), F32) for _ in range(8)]
    for e in range(FAR2):
        which = jnp.broadcast_to(listed[:, 64 + FAR2 + e : 65 + FAR2 + e], (D, 128)) - odd
        term = picked[e * D : (e + 1) * D]
        for t in range(8):
            z[t] = z[t] + jnp.where(which == 2.0 * t, term, 0.0)
    total = jnp.zeros((2 * D, 128), F32)
    for u in range(4):
        hi, lo = halves(jnp.concatenate(z[2 * u : 2 * u + 2], axis=1))
        total = total + bnt(jnp.concatenate([hi, lo], axis=0), table[u])
    hi, lo = halves(total[:D, :64] + total[:D, 64:] + total[D:, :64])
    spread = bnt(hi, down[0]) + (bnt(lo, down[0]) + bnt(hi, down[1]))
    for t in range(4):
        out_ref[:, 0, t * 128 : (t + 1) * 128] = fine_ref[t] + spread[:, t * 128 : (t + 1) * 128]


def product_kernel(got_ref, near_ref, v_ref, b_ref, out_ref, gram_ref, buf):
    got = dense(got_ref, buf)
    for b in range(C):
        cols = slice(b * M, (b + 1) * M)
        lanes = slice((b % 4) * R, (b % 4 + 1) * R)
        local = jnp.concatenate([got[b // 4][:, lanes], got[2 + b // 4][:, lanes]], axis=0)
        out_ref[:, cols] = near_ref[:, cols] + nn(local, b_ref[:, cols])
    v = v_ref[...]
    image = out_ref[...]
    for k, g in enumerate((nt(v, v), nt(v, image), nt(image, image))):
        gram_ref[:, 0, k * 128 : (k + 1) * 128] = jnp.concatenate([g[:D], g[D:]], axis=1)


def row_of(x, mask):
    return jnp.broadcast_to(jnp.sum(jnp.where(mask, x, 0.0), axis=0, keepdims=True), (8, 128))


def finish_kernel(got_ref, v_ref, p_ref, next_ref, hess_ref, factor_ref, buf):
    panels = float(M * C * D * 16)
    basis, mixed, image = [jnp.concatenate([g[:, :64], g[:, 64:]], axis=0) for g in dense(got_ref, buf)]
    hess = mixed * (1.0 / panels)
    hess_ref[...] = hess
    cross = tn(mixed, hess)
    gram = (image - cross - jnp.transpose(cross) + nn(tn(hess, basis), hess)) * (1.0 / panels)
    residual = p_ref[...] - tn(hess, v_ref[...])
    row = lax.broadcasted_iota(jnp.int32, (Q, Q), 0)
    col = lax.broadcasted_iota(jnp.int32, (Q, Q), 1)
    work = jnp.concatenate([gram, jnp.where(row == col, 1.0, 0.0)], axis=1)
    tiles = [work[8 * k : 8 * k + 8] for k in range(8)]
    sub = lax.broadcasted_iota(jnp.int32, (8, 128), 0)
    scales = [jnp.zeros((8, 128), F32) for _ in range(8)]
    for j in range(0, Q, 2):
        own = j // 8
        at = j % 8
        tile = tiles[own]
        first = jnp.broadcast_to(tile[:, j : j + 1], (8, 128))
        second = jnp.broadcast_to(tile[:, j + 1 : j + 2], (8, 128))
        line = jnp.broadcast_to(tile[at : at + 1], (8, 128))
        following = jnp.broadcast_to(tile[at + 1 : at + 2], (8, 128))
        corner = row_of(first, sub == at)
        right = row_of(second, sub == at)
        below = row_of(first, sub == at + 1)
        pivot = row_of(second, sub == at + 1)
        inverse = 1.0 / corner
        ratio = below * inverse
        across = right * inverse
        pivot = pivot - ratio * right
        following = following - ratio * line
        line = line * inverse
        scaled = following * (1.0 / pivot)
        scales[own] = jnp.where(sub == at, corner, jnp.where(sub == at + 1, pivot, scales[own]))
        if at < 6:
            lower = tile - first * line - (second - first * across) * scaled
            tiles[own] = jnp.where(sub > at + 1, lower, jnp.where(sub == at + 1, following, tile))
        else:
            tiles[own] = jnp.where(sub == at + 1, following, tile)
        for k in range(own + 1, 8):
            first = jnp.broadcast_to(tiles[k][:, j : j + 1], (8, 128))
            second = jnp.broadcast_to(tiles[k][:, j + 1 : j + 2], (8, 128))
            tiles[k] = tiles[k] - first * line - (second - first * across) * scaled
    whole = jnp.concatenate([tiles[k] * lax.rsqrt(scales[k]) for k in range(8)], axis=0)
    factor_ref[...] = jnp.transpose(jnp.where(col >= row, whole[:, :Q], 0.0))
    next_ref[...] = nn(whole[:, Q:], residual)


def sds(*shape):
    return jax.ShapeDtypeStruct(shape, F32)


def bds(*shape):
    return jax.ShapeDtypeStruct(shape, BF16)


SMEM = pl.BlockSpec(memory_space=pltpu.SMEM)
VMEM = pl.BlockSpec(memory_space=pltpu.VMEM)


def call(kernel, out, smem=0, vmem=0, scratch=()):
    return pl.pallas_call(
        kernel,
        out_shape=out,
        in_specs=[SMEM] * smem + [VMEM] * vmem,
        out_specs=jax.tree.map(lambda _: VMEM, out),
        scratch_shapes=list(scratch),
        compiler_params=pltpu.CompilerParams(vmem_limit_bytes=16 << 20),
    )


def exchange(blocks, axes):
    return lax.all_to_all(blocks, axes, 0, 0, tiled=True)


def step(
    krylov_block,
    bases,
    points,
    panel_size,
    panel_weight,
    near_list,
    far_list,
    far_class,
    far_count,
    coarse_list,
    coarse_class,
    coarse_count,
    couple_fine,
    couple_coarse,
    up_transfer,
    down_transfer,
):
    sent, own = pl.pallas_call(
        poles_kernel,
        out_shape=(sds(D, 1, 896), sds(Q + 8, W)),
        in_specs=[pl.BlockSpec(memory_space=pltpu.HBM)] * 12,
        out_specs=(VMEM, VMEM),
        scratch_shapes=[
            pltpu.SMEM((C,), jnp.int32),
            pltpu.SMEM((1,), jnp.int32),
            pltpu.VMEM((R, W), F32),
            pltpu.VMEM((C, R, R), F32),
            pltpu.VMEM((C, FAR1), jnp.int32),
            pltpu.VMEM((C, FAR1), jnp.int32),
            pltpu.VMEM((1, FAR2), jnp.int32),
            pltpu.VMEM((1, FAR2), jnp.int32),
            pltpu.SemaphoreType.DMA((12,)),
        ],
        name="poles",
    )(
        far_count,
        coarse_count,
        krylov_block,
        bases,
        up_transfer,
        far_list,
        far_class,
        coarse_list,
        coarse_class,
        points,
        panel_size[None],
        panel_weight[None],
    )
    inner = lax.ppermute(own, BOX, [(i, i ^ 1) for i in range(D)])
    outer = lax.ppermute(own, BOX, [(i, ((i + 1) ^ 1) - 1) for i in range(1, D - 1)])
    got = exchange(sent, BOX)
    fine_table, coarse_table, down_table = call(
        tables_kernel, (bds(4, 128, 256), bds(4, 128, 256), bds(2, 2 * C * R, 2 * R)), 0, 3
    )(couple_fine, couple_coarse, down_transfer)
    near = pl.pallas_call(
        near_kernel,
        out_shape=sds(Q, W),
        in_specs=[pl.BlockSpec(memory_space=pltpu.HBM)] + [VMEM] * 3,
        out_specs=VMEM,
        scratch_shapes=[
            pltpu.SMEM((C, NEAR), jnp.int32),
            pltpu.SemaphoreType.DMA,
            pltpu.VMEM((C, M, 8), F32),
            pltpu.VMEM((4, M, M), F32),
            pltpu.VMEM((4, M, M), F32),
            pltpu.VMEM((3 * C, Q, M), BF16),
            pltpu.VMEM((3 * C, Q, M), BF16),
            pltpu.VMEM((3 * C, 4, M), F32),
        ],
        compiler_params=pltpu.CompilerParams(vmem_limit_bytes=16 << 20),
        name="near",
    )(near_list, inner, own, outer)
    got, near, fine_table, coarse_table, down_table = lax.optimization_barrier(
        (got, near, fine_table, coarse_table, down_table)
    )
    coarse_all = exchange(call(coarse_send_kernel, sds(16, 16, 128), 0, 1, [pltpu.VMEM((D, 128), F32)])(got), LEAF)
    fine = call(
        fine_kernel,
        sds(4, D, 128),
        0,
        2,
        [pltpu.VMEM((4, C * D, 256), BF16), pltpu.VMEM((4, C * D, 256), BF16), pltpu.VMEM((7, D, 128), F32)],
    )(got, fine_table)
    back = call(coarse_kernel, sds(D, 1, 512), 0, 5, [pltpu.VMEM((D, 128), F32)])(
        got, coarse_all, coarse_table, down_table, fine
    )
    local = exchange(back, BOX)
    product, grams = call(product_kernel, (sds(Q, W), sds(D, 1, 384)), 0, 4, [pltpu.VMEM((4, D, 128), F32)])(
        local, near, krylov_block, bases
    )
    part = jnp.sum(exchange(grams, PLANE), axis=0)
    part = exchange(jnp.broadcast_to(part[None], (16, 1, 384)), "box_0")
    part = jnp.sum(part, axis=0)
    whole = exchange(jnp.broadcast_to(part[None], (D, 1, 384)), PLANE)
    return call(finish_kernel, (sds(Q, W), sds(Q, Q), sds(Q, Q)), 0, 3, [pltpu.VMEM((3, D, 128), F32)])(
        whole, krylov_block, product
    )


def solution(mesh):
    split = Mesh(mesh.devices.reshape(4, 4, 16, 2), LEAF_BOX)
    placed = (
        P(None, LEAF_BOX),
        P(None, LEAF_BOX),
        P(None, LEAF_BOX),
        P(LEAF_BOX),
        P(LEAF_BOX),
        P(LEAF_BOX, None),
        P(LEAF_BOX, None),
        P(LEAF_BOX, None),
        P(LEAF_BOX),
        P(LEAF_BOX, None),
        P(LEAF_BOX, None),
        P(LEAF_BOX),
        P(),
        P(),
        P(),
        P(),
    )
    return jax.shard_map(
        step,
        mesh=split,
        in_specs=placed,
        out_specs=(P(None, LEAF_BOX), P(), P()),
        check_vma=False,
    )
```

```python
import jax
import jax.numpy as jnp
from jax import lax
from jax.experimental import pallas as pl
from jax.experimental.pallas import tpu as pltpu
from jax.sharding import Mesh
from jax.sharding import PartitionSpec as P

LEAF = ("leaf_0", "leaf_1")
BOX = ("box_0", "box_1")
LEAF_BOX = LEAF + BOX
PLANE = ("leaf_0", "leaf_1", "box_1")
F32 = jnp.float32
BF16 = jnp.bfloat16
HI = lax.Precision.HIGHEST
NT = (((1,), (1,)), ((), ()))
TN = (((0,), (0,)), ((), ()))

Q = 64
R = 32
M = 128
C = 8
NEAR = 16
FAR1 = 12
FAR2 = 16
D = 32
W = C * M


def nn(a, b):
    return jnp.dot(a, b, precision=HI, preferred_element_type=F32)


def nt(a, b):
    return lax.dot_general(a, b, NT, precision=HI, preferred_element_type=F32)


def tn(a, b):
    return lax.dot_general(a, b, TN, precision=HI, preferred_element_type=F32)


def bdot(a, b):
    return jnp.dot(a, b, preferred_element_type=F32)


def bnt(a, b):
    return lax.dot_general(a, b, NT, preferred_element_type=F32)


def halves(x):
    hi = x.astype(BF16)
    return hi, (x - hi.astype(F32)).astype(BF16)


def dense(ref, buf):
    for k in range(buf.shape[0]):
        buf[k] = ref[:, 0, k * 128 : (k + 1) * 128]
    return [buf[k] for k in range(buf.shape[0])]


def lane_flat(x, rows, width):
    wide = jnp.concatenate([x] * rows + [jnp.zeros((rows, 128 - rows * width), F32)], axis=1)
    lane = lax.broadcasted_iota(jnp.int32, (rows, 128), 1)
    row = lax.broadcasted_iota(jnp.int32, (rows, 128), 0)
    keep = (lane >= row * width) & (lane < (row + 1) * width)
    return jnp.sum(jnp.where(keep, wide, 0.0), axis=0, keepdims=True)


def poles_kernel(*refs):
    sources = refs[:12]
    out_ref, own = refs[12:14]
    own[Q : Q + 8, :] = jnp.zeros((8, W), F32)
    places = list(refs[14:16]) + [own.at[pl.ds(0, Q)]] + list(refs[16:22])
    places += [own.at[pl.ds(Q, 3)], own.at[pl.ds(Q + 3, 1)], own.at[pl.ds(Q + 4, 1)]]
    copies = [pltpu.make_async_copy(x, y, refs[22].at[k]) for k, (x, y) in enumerate(zip(sources, places))]
    for copy in copies:
        copy.start()
    for copy in copies:
        copy.wait()
    far_count, coarse_count, b_ref, up_ref, far_list, far_class, coarse_list, coarse_class = refs[14:22]
    v_ref = own
    parts = []
    coarse = jnp.zeros((Q, R), F32)
    for b in range(C):
        cols = slice(b * M, (b + 1) * M)
        vhi, vlo = halves(v_ref[:Q, cols])
        bhi, blo = halves(b_ref[:, cols])
        both = bnt(jnp.concatenate([vhi, vlo], axis=0), bhi)
        pole = both[:Q] + (both[Q:] + bnt(vhi, blo))
        parts.append(pole)
    for b in range(C):
        phi, plo = halves(parts[b])
        uhi, ulo = halves(up_ref[b])
        both = bdot(jnp.concatenate([phi, plo], axis=0), uhi)
        coarse = coarse + (both[:Q] + (both[Q:] + bdot(phi, ulo)))
    for half in range(2):
        rows = slice(half * D, (half + 1) * D)
        for t in range(2):
            out_ref[:, 0, (2 * half + t) * 128 : (2 * half + t + 1) * 128] = jnp.concatenate([p[rows] for p in parts[4 * t : 4 * t + 4]], axis=1)
    slot = lax.broadcasted_iota(jnp.int32, (C, FAR1), 1)
    row = lax.broadcasted_iota(jnp.int32, (C, FAR1), 0)
    live = jnp.zeros((C, FAR1), jnp.int32)
    for b in range(C):
        live = jnp.where(row == b, far_count[b], live)
    box = far_list[...] & 255
    place = ((box & 7) * D + (box >> 3)).astype(F32)
    place = jnp.where(slot < live, place, -1.0)
    out_ref[:, 0, 640:768] = jnp.broadcast_to(lane_flat(place, C, FAR1), (D, 128))
    out_ref[:, 0, 768:896] = jnp.broadcast_to(lane_flat(far_class[...].astype(F32), C, FAR1), (D, 128))
    parent = coarse_list[...]
    inner = parent & 31
    spot = ((parent >> 5) * 16 + (inner & 15) + (inner >> 4) * 256).astype(F32)
    spot = jnp.where(lax.broadcasted_iota(jnp.int32, (1, FAR2), 1) < coarse_count[0], spot, -1.0)
    tail = jnp.concatenate(
        [spot, coarse_class[...].astype(F32), jnp.zeros((1, 128 - 64 - 2 * FAR2), F32)], axis=1
    )
    out_ref[:, 0, 512:640] = jnp.concatenate(
        [coarse[:D], coarse[D:], jnp.broadcast_to(tail, (D, 64))], axis=1
    )


def spread(out, columns):
    for k in range(4):
        out[k] = jnp.broadcast_to(columns[:, k : k + 1], (M, M))


def near_kernel(listed, inner, own, outer, out_ref, index, sem, turned, even, odd, vhi, vlo, rows):
    copy = pltpu.make_async_copy(listed, index, sem)
    copy.start()
    for part, ref in enumerate((inner, own, outer)):
        for s in range(C):
            cols = slice(s * M, (s + 1) * M)
            rows[part * C + s] = ref[Q : Q + 4, cols]
            value = ref[:Q, cols] * (ref[Q + 4 : Q + 5, cols] * (1.0 / (M * NEAR)))
            hi, lo = halves(value)
            vhi[part * C + s] = hi
            vlo[part * C + s] = lo
    for s in range(C):
        turned[s] = jnp.transpose(own[Q : Q + 8, s * M : (s + 1) * M])
    spread(even, turned[0])
    copy.wait()
    base = index[0, 0] - C
    flip = 16 * (1 - ((index[0, 0] >> 3) & 1))

    def one_box(b, geo, ahead):
        acc = jnp.zeros((Q, M), F32)
        for pair in range(NEAR // 2):
            ghi = []
            glo = []
            at = [index[b, 2 * pair + k] - base for k in range(2)]
            at = [i + flip * (1 - (i >> 3)) for i in at]
            for i in at:
                d0 = geo[0] - rows[i, 0:1]
                d1 = geo[1] - rows[i, 1:2]
                d2 = geo[2] - rows[i, 2:3]
                g = lax.rsqrt(d0 * d0 + d1 * d1 + d2 * d2 + geo[3] * rows[i, 3:4])
                hi, lo = halves(g)
                ghi.append(hi)
                glo.append(lo)
            ghi = jnp.concatenate(ghi, axis=1)
            glo = jnp.concatenate(glo, axis=1)
            xhi = jnp.concatenate([vhi[i] for i in at], axis=1)
            xlo = jnp.concatenate([vlo[i] for i in at], axis=1)
            both = bnt(jnp.concatenate([xhi, xlo], axis=0), ghi)
            acc = acc + (both[:Q] + (both[Q:] + bnt(xhi, glo)))
        out_ref[:, pl.ds(pl.multiple_of(b * M, M), M)] = acc
        spread(ahead, turned[(b + 1) & 7])

    def two_boxes(i, carry):
        one_box(2 * i, even, odd)
        one_box(2 * i + 1, odd, even)
        return carry

    lax.fori_loop(0, C // 2, two_boxes, 0)


def coarse_send_kernel(got_ref, out_ref, buf):
    buf[...] = got_ref[:, 0, 512:640]
    pole = buf[...]
    both = jnp.concatenate([pole[:16, :64], pole[16:, :64]], axis=1)
    for k in range(16):
        out_ref[k] = both


def doubled(x):
    return x + pltpu.roll(x, 64, 1)


def tables_kernel(fine, coarse, down, fine_out, coarse_out, down_out):
    zero = jnp.zeros((R, R), F32)
    for table, out in ((fine, fine_out), (coarse, coarse_out)):
        for u in range(4):
            top = []
            low = []
            for k in range(4):
                top += [table[4 * u + k], zero]
                low += [zero, table[4 * u + k]]
            hi, lo = halves(jnp.concatenate([jnp.concatenate(top, axis=1), jnp.concatenate(low, axis=1)], axis=0))
            out[u] = jnp.concatenate([hi, lo], axis=0)
    rows = [jnp.concatenate([down[j], zero], axis=1) for j in range(C)]
    rows += [jnp.concatenate([zero, down[j]], axis=1) for j in range(C)]
    hi, lo = halves(jnp.concatenate(rows, axis=0))
    down_out[0] = hi
    down_out[1] = lo


def fine_kernel(got_ref, table, out_ref, zhi, zlo, buf):
    got = dense(got_ref, buf)
    pieces = []
    for j in range(C):
        lanes = slice((j % 4) * R, (j % 4 + 1) * R)
        pieces.append(jnp.concatenate([got[j // 4][:, lanes], got[2 + j // 4][:, lanes]], axis=1))
    hi, lo = halves(jnp.concatenate(pieces, axis=0))
    source = jnp.concatenate([hi, lo], axis=1)
    place = got[5]
    kind = got[6]
    lane = lax.broadcasted_iota(jnp.int32, (D, C * D), 1).astype(F32)
    odd = (lax.broadcasted_iota(jnp.int32, (D, 128), 1) >= 64).astype(F32)
    for j in range(C):
        hot = []
        for e in range(FAR1):
            k = j * FAR1 + e
            hot.append(jnp.where(jnp.broadcast_to(place[:, k : k + 1], (D, C * D)) == lane, 1.0, 0.0))
        picked = doubled(bdot(jnp.concatenate(hot, axis=0).astype(BF16), source))
        z = [jnp.zeros((D, 128), F32) for _ in range(8)]
        for e in range(FAR1):
            k = j * FAR1 + e
            which = jnp.broadcast_to(kind[:, k : k + 1], (D, 128)) - odd
            term = picked[e * D : (e + 1) * D]
            for t in range(8):
                z[t] = z[t] + jnp.where(which == 2.0 * t, term, 0.0)
        for t in range(8):
            hi, lo = halves(z[t])
            zhi[t // 2, j * D : (j + 1) * D, (t % 2) * 128 : (t % 2 + 1) * 128] = hi
            zlo[t // 2, j * D : (j + 1) * D, (t % 2) * 128 : (t % 2 + 1) * 128] = lo
    total = jnp.zeros((C * D, 128), F32)
    extra = jnp.zeros((C * D, 64), F32)
    for u in range(4):
        total = total + bnt(zhi[u], table[u])
        extra = extra + bnt(zlo[u], table[u, :64])
    total = total[:, :64] + total[:, 64:] + extra
    for q in range(2):
        for h in range(2):
            out_ref[2 * q + h] = jnp.concatenate(
                [total[(4 * h + k) * D : (4 * h + k + 1) * D, q * R : (q + 1) * R] for k in range(4)], axis=1
            )


def coarse_kernel(got_ref, all_ref, table, down, fine_ref, out_ref, buf):
    hi, lo = halves(all_ref[...].reshape(256, 128))
    source = jnp.concatenate(
        [
            jnp.concatenate([hi[:, :64], lo[:, :64]], axis=1),
            jnp.concatenate([hi[:, 64:], lo[:, 64:]], axis=1),
        ],
        axis=0,
    )
    buf[...] = got_ref[:, 0, 512:640]
    listed = buf[...]
    lane = lax.broadcasted_iota(jnp.int32, (D, 512), 1).astype(F32)
    hot = [
        jnp.where(jnp.broadcast_to(listed[:, 64 + e : 65 + e], (D, 512)) == lane, 1.0, 0.0)
        for e in range(FAR2)
    ]
    picked = doubled(bdot(jnp.concatenate(hot, axis=0).astype(BF16), source))
    odd = (lax.broadcasted_iota(jnp.int32, (D, 128), 1) >= 64).astype(F32)
    z = [jnp.zeros((D, 128), F32) for _ in range(8)]
    for e in range(FAR2):
        which = jnp.broadcast_to(listed[:, 64 + FAR2 + e : 65 + FAR2 + e], (D, 128)) - odd
        term = picked[e * D : (e + 1) * D]
        for t in range(8):
            z[t] = z[t] + jnp.where(which == 2.0 * t, term, 0.0)
    total = jnp.zeros((2 * D, 128), F32)
    for u in range(4):
        hi, lo = halves(jnp.concatenate(z[2 * u : 2 * u + 2], axis=1))
        total = total + bnt(jnp.concatenate([hi, lo], axis=0), table[u])
    hi, lo = halves(total[:D, :64] + total[:D, 64:] + total[D:, :64])
    spread = bnt(hi, down[0]) + (bnt(lo, down[0]) + bnt(hi, down[1]))
    for t in range(4):
        out_ref[:, 0, t * 128 : (t + 1) * 128] = fine_ref[t] + spread[:, t * 128 : (t + 1) * 128]


def product_kernel(got_ref, near_ref, v_ref, b_ref, out_ref, gram_ref, buf):
    got = dense(got_ref, buf)
    for b in range(C):
        cols = slice(b * M, (b + 1) * M)
        lanes = slice((b % 4) * R, (b % 4 + 1) * R)
        local = jnp.concatenate([got[b // 4][:, lanes], got[2 + b // 4][:, lanes]], axis=0)
        out_ref[:, cols] = near_ref[:, cols] + nn(local, b_ref[:, cols])
    v = v_ref[...]
    image = out_ref[...]
    for k, g in enumerate((nt(v, v), nt(v, image), nt(image, image))):
        gram_ref[:, 0, k * 128 : (k + 1) * 128] = jnp.concatenate([g[:D], g[D:]], axis=1)


def row_of(x, mask):
    return jnp.broadcast_to(jnp.sum(jnp.where(mask, x, 0.0), axis=0, keepdims=True), (8, 128))


def finish_kernel(got_ref, v_ref, p_ref, next_ref, hess_ref, factor_ref, buf):
    panels = float(M * C * D * 16)
    basis, mixed, image = [jnp.concatenate([g[:, :64], g[:, 64:]], axis=0) for g in dense(got_ref, buf)]
    hess = mixed * (1.0 / panels)
    hess_ref[...] = hess
    cross = tn(mixed, hess)
    gram = (image - cross - jnp.transpose(cross) + nn(tn(hess, basis), hess)) * (1.0 / panels)
    residual = p_ref[...] - tn(hess, v_ref[...])
    row = lax.broadcasted_iota(jnp.int32, (Q, Q), 0)
    col = lax.broadcasted_iota(jnp.int32, (Q, Q), 1)
    work = jnp.concatenate([gram, jnp.where(row == col, 1.0, 0.0)], axis=1)
    tiles = [work[8 * k : 8 * k + 8] for k in range(8)]
    sub = lax.broadcasted_iota(jnp.int32, (8, 128), 0)
    scales = [jnp.zeros((8, 128), F32) for _ in range(8)]
    for j in range(0, Q, 2):
        own = j // 8
        at = j % 8
        tile = tiles[own]
        first = jnp.broadcast_to(tile[:, j : j + 1], (8, 128))
        second = jnp.broadcast_to(tile[:, j + 1 : j + 2], (8, 128))
        line = jnp.broadcast_to(tile[at : at + 1], (8, 128))
        following = jnp.broadcast_to(tile[at + 1 : at + 2], (8, 128))
        corner = row_of(first, sub == at)
        right = row_of(second, sub == at)
        below = row_of(first, sub == at + 1)
        pivot = row_of(second, sub == at + 1)
        inverse = 1.0 / corner
        ratio = below * inverse
        across = right * inverse
        pivot = pivot - ratio * right
        following = following - ratio * line
        line = line * inverse
        scaled = following * (1.0 / pivot)
        scales[own] = jnp.where(sub == at, corner, jnp.where(sub == at + 1, pivot, scales[own]))
        if at < 6:
            lower = tile - first * line - (second - first * across) * scaled
            tiles[own] = jnp.where(sub > at + 1, lower, jnp.where(sub == at + 1, following, tile))
        else:
            tiles[own] = jnp.where(sub == at + 1, following, tile)
        for k in range(own + 1, 8):
            first = jnp.broadcast_to(tiles[k][:, j : j + 1], (8, 128))
            second = jnp.broadcast_to(tiles[k][:, j + 1 : j + 2], (8, 128))
            tiles[k] = tiles[k] - first * line - (second - first * across) * scaled
    whole = jnp.concatenate([tiles[k] * lax.rsqrt(scales[k]) for k in range(8)], axis=0)
    factor_ref[...] = jnp.transpose(jnp.where(col >= row, whole[:, :Q], 0.0))
    next_ref[...] = nn(whole[:, Q:], residual)


def sds(*shape):
    return jax.ShapeDtypeStruct(shape, F32)


def bds(*shape):
    return jax.ShapeDtypeStruct(shape, BF16)


SMEM = pl.BlockSpec(memory_space=pltpu.SMEM)
VMEM = pl.BlockSpec(memory_space=pltpu.VMEM)


def call(kernel, out, smem=0, vmem=0, scratch=()):
    return pl.pallas_call(
        kernel,
        out_shape=out,
        in_specs=[SMEM] * smem + [VMEM] * vmem,
        out_specs=jax.tree.map(lambda _: VMEM, out),
        scratch_shapes=list(scratch),
        compiler_params=pltpu.CompilerParams(vmem_limit_bytes=16 << 20),
    )


def exchange(blocks, axes):
    return lax.all_to_all(blocks, axes, 0, 0, tiled=True)


def step(
    krylov_block,
    bases,
    points,
    panel_size,
    panel_weight,
    near_list,
    far_list,
    far_class,
    far_count,
    coarse_list,
    coarse_class,
    coarse_count,
    couple_fine,
    couple_coarse,
    up_transfer,
    down_transfer,
):
    sent, own = pl.pallas_call(
        poles_kernel,
        out_shape=(sds(D, 1, 896), sds(Q + 8, W)),
        in_specs=[pl.BlockSpec(memory_space=pltpu.HBM)] * 12,
        out_specs=(VMEM, VMEM),
        scratch_shapes=[
            pltpu.SMEM((C,), jnp.int32),
            pltpu.SMEM((1,), jnp.int32),
            pltpu.VMEM((R, W), F32),
            pltpu.VMEM((C, R, R), F32),
            pltpu.VMEM((C, FAR1), jnp.int32),
            pltpu.VMEM((C, FAR1), jnp.int32),
            pltpu.VMEM((1, FAR2), jnp.int32),
            pltpu.VMEM((1, FAR2), jnp.int32),
            pltpu.SemaphoreType.DMA((12,)),
        ],
        compiler_params=pltpu.CompilerParams(vmem_limit_bytes=16 << 20),
        name="poles",
    )(
        pltpu.with_memory_space_constraint(far_count, pltpu.HBM),
        coarse_count,
        *[
            pltpu.with_memory_space_constraint(x, pltpu.HBM)
            for x in (
                krylov_block,
                bases,
                up_transfer,
                far_list,
                far_class,
                coarse_list,
                coarse_class,
                points,
                panel_size[None],
                panel_weight[None],
            )
        ]
    )
    inner = lax.ppermute(own, BOX, [(i, i ^ 1) for i in range(D)])
    outer = lax.ppermute(own, BOX, [(i, ((i + 1) ^ 1) - 1) for i in range(1, D - 1)])
    got = exchange(sent, BOX)
    fine_table, coarse_table, down_table = call(
        tables_kernel, (bds(4, 128, 256), bds(4, 128, 256), bds(2, 2 * C * R, 2 * R)), 0, 3
    )(couple_fine, couple_coarse, down_transfer)
    near = pl.pallas_call(
        near_kernel,
        out_shape=sds(Q, W),
        in_specs=[pl.BlockSpec(memory_space=pltpu.HBM)] + [VMEM] * 3,
        out_specs=VMEM,
        scratch_shapes=[
            pltpu.SMEM((C, NEAR), jnp.int32),
            pltpu.SemaphoreType.DMA,
            pltpu.VMEM((C, M, 8), F32),
            pltpu.VMEM((4, M, M), F32),
            pltpu.VMEM((4, M, M), F32),
            pltpu.VMEM((3 * C, Q, M), BF16),
            pltpu.VMEM((3 * C, Q, M), BF16),
            pltpu.VMEM((3 * C, 4, M), F32),
        ],
        compiler_params=pltpu.CompilerParams(vmem_limit_bytes=16 << 20),
        name="near",
    )(near_list, inner, own, outer)
    got, near, fine_table, coarse_table, down_table = lax.optimization_barrier(
        (got, near, fine_table, coarse_table, down_table)
    )
    coarse_all = exchange(call(coarse_send_kernel, sds(16, 16, 128), 0, 1, [pltpu.VMEM((D, 128), F32)])(got), LEAF)
    fine = call(
        fine_kernel,
        sds(4, D, 128),
        0,
        2,
        [pltpu.VMEM((4, C * D, 256), BF16), pltpu.VMEM((4, C * D, 256), BF16), pltpu.VMEM((7, D, 128), F32)],
    )(got, fine_table)
    back = call(coarse_kernel, sds(D, 1, 512), 0, 5, [pltpu.VMEM((D, 128), F32)])(
        got, coarse_all, coarse_table, down_table, fine
    )
    local = exchange(back, BOX)
    product, grams = call(product_kernel, (sds(Q, W), sds(D, 1, 384)), 0, 4, [pltpu.VMEM((4, D, 128), F32)])(
        local, near, krylov_block, bases
    )
    part = jnp.sum(exchange(grams, PLANE), axis=0)
    part = exchange(jnp.broadcast_to(part[None], (16, 1, 384)), "box_0")
    part = jnp.sum(part, axis=0)
    whole = exchange(jnp.broadcast_to(part[None], (D, 1, 384)), PLANE)
    return call(finish_kernel, (sds(Q, W), sds(Q, Q), sds(Q, Q)), 0, 3, [pltpu.VMEM((3, D, 128), F32)])(
        whole, krylov_block, product
    )


def solution(mesh):
    split = Mesh(mesh.devices.reshape(4, 4, 16, 2), LEAF_BOX)
    placed = (
        P(None, LEAF_BOX),
        P(None, LEAF_BOX),
        P(None, LEAF_BOX),
        P(LEAF_BOX),
        P(LEAF_BOX),
        P(LEAF_BOX, None),
        P(LEAF_BOX, None),
        P(LEAF_BOX, None),
        P(LEAF_BOX),
        P(LEAF_BOX, None),
        P(LEAF_BOX, None),
        P(LEAF_BOX),
        P(),
        P(),
        P(),
        P(),
    )
    return jax.shard_map(
        step,
        mesh=split,
        in_specs=placed,
        out_specs=(P(None, LEAF_BOX), P(), P()),
        check_vma=False,
    )
```
